128 devices in a mesh: space: 32 (over x, z, core), rep: 4 (over y).
Axes of the slice: x: 4, y: 4, z: 4, core: 2. Of those that a mesh axis runs over, the one named last changes fastest.
Arguments:
- atom_features: float32 [131072, 64], P('space'), may hold values from -6 to 6
- bond_features: bfloat16 [131072, 1024], P(('space', 'rep')), may hold values from -6 to 6
- offsets: int32 [131072, 16], P(('space', 'rep')), may hold values from -2048 to 2048, as said below
- counts: int32 [131072], P(('space', 'rep')), may hold values from 8 to 16
- cosines: float32 [131072, 256], P(('space', 'rep')), may hold values from -1 to 1
- weight_core: bfloat16 [2, 192, 192], replicated, may hold values from -0.4375 to 0.4375
- weight_atom: bfloat16 [2, 64, 64], replicated, may hold values from -0.75 to 0.75
- weight_pair: bfloat16 [2, 64, 128], replicated, may hold values from -0.75 to 0.75
- weight_cosine: float32 [2, 64], replicated, may hold values from -6 to 6
- weight_bond: bfloat16 [2, 64, 64], replicated, may hold values from -0.75 to 0.75
- weight_energy: float32 [64], replicated, may hold values from -0.75 to 0.75
Outputs:
- atoms_out: float32 [131072, 64], P(('space', 'rep'))
- bonds_out: bfloat16 [131072, 1024], P(('space', 'rep'))
- energy: float32 [], replicated
The draws below stay inside these ranges and needn't reach their ends.
Inputs may be any that keep to these rules, and one draw needn't show every extreme that they name: `offsets`: never zero; |offset| is at most 2048.
All inputs are finite; a program needn't handle non-finite values.
Results may differ from the reference program's by a relative error of at most 0.0045.
Values may be sent and summed in bfloat16 or wider, within the bound.
A program may use at most 64 MiB of HBM per device.

```python
import math
import jax
import jax.numpy as jnp
from jax import lax

C = 64
SLOT = 16
LAYERS = 2
HALO = 2048
ATOMS = 131072


def draw_offsets(key, part):
    first, second = jax.random.split(jax.random.fold_in(key, 7))
    magnitude = jax.random.randint(first, (ATOMS, SLOT), 1, HALO + 1, dtype=jnp.int32)
    signs = jax.random.randint(second, (ATOMS, SLOT), 0, 2, dtype=jnp.int32) * 2 - 1
    return (magnitude * signs).astype(jnp.int32)


def touch_ends(result, own_key, least, largest):
    longest = result.shape.index(max(result.shape))
    spots = []
    for shift in (0, 1):
        where = [jax.random.randint(jax.random.fold_in(own_key, axis), (), 0, length) for axis, length in enumerate(result.shape)]
        where[longest] = (where[longest] + shift) % result.shape[longest]
        spots.append(tuple(where))
    return result.at[spots[0]].set(least).at[spots[1]].set(largest)


def shard_levels(rng, dims, shards, smallest, largest):
    def one(axis_at, parts):
        steps = jax.random.uniform(jax.random.fold_in(jax.random.fold_in(rng, 6), axis_at), (parts,), jnp.float32, smallest / len(shards), largest / len(shards))
        return jnp.repeat(jnp.exp(steps), dims[axis_at] // parts).reshape((-1,) + (1,) * (len(dims) - axis_at - 1))

    loudness = one(*shards[0])
    for cut in shards[1:]:
        loudness = loudness * one(*cut)
    return loudness


def noise(own_key, shape, deviation, bound, shards=(), held_as=jnp.bfloat16):
    gain = shard_levels(own_key, shape, shards, -0.22, 0.18) if shards else 1.0
    entries = jax.random.normal(own_key, shape, jnp.float32) * deviation * gain
    return jnp.minimum(jnp.maximum(entries, -bound), bound).astype(held_as)


def setup_inputs(seed: int = 0) -> dict:
    key_of = jax.random.split(jax.random.key(seed), 12)
    return {
        "atom_features": noise(key_of[0], (ATOMS, C), 1.0, 6.0, ((0, 32),), jnp.float32),
        "bond_features": noise(key_of[1], (ATOMS, SLOT * C), 1.0, 6.0, ((0, 128),)),
        "offsets": draw_offsets(jax.random.fold_in(key_of[11], 71), 0),
        "counts": touch_ends(jax.random.randint(key_of[3], (ATOMS,), 8, 17), jax.random.fold_in(key_of[3], 1), 8, 16).astype(jnp.int32),
        "cosines": jnp.clip(jax.random.uniform(key_of[4], (ATOMS, SLOT * SLOT), jnp.float32, -1.0, 1.0) * shard_levels(key_of[4], (ATOMS, SLOT * SLOT), ((0, 128),), -0.4, 0.0), -1.0, 1.0),
        "weight_core": noise(key_of[5], (LAYERS, 3 * C, 3 * C), (3 * C) ** -0.5, 0.4375),
        "weight_atom": noise(key_of[6], (LAYERS, C, C), C ** -0.5, 0.75),
        "weight_pair": noise(key_of[7], (LAYERS, C, 2 * C), C ** -0.5, 0.75),
        "weight_cosine": noise(key_of[8], (LAYERS, C), 1.0, 6.0, (), jnp.float32),
        "weight_bond": noise(key_of[9], (LAYERS, C, C), C ** -0.5, 0.75),
        "weight_energy": noise(key_of[10], (C,), C ** -0.5, 0.75, (), jnp.float32),
    }


def interact(h_rows, neighbours, e_rows, cnt_rows, cos_rows, weight_core, weight_atom, weight_pair, weight_cosine, weight_bond):
    row_count = h_rows.shape[0]
    channels = h_rows.shape[1]
    slot_count = e_rows.shape[1] // channels
    bond_rows = e_rows.reshape(row_count, slot_count, channels)
    centre = jnp.broadcast_to(h_rows.astype(jnp.bfloat16)[:, None, :], (row_count, slot_count, channels))
    joined = jnp.concatenate([centre, neighbours, bond_rows], axis=2).reshape(row_count * slot_count, 3 * channels)
    mixed_all = jnp.dot(joined, weight_core, preferred_element_type=jnp.float32).reshape(row_count, slot_count, 3 * channels)
    live_mask = (jnp.arange(slot_count, dtype=jnp.int32)[None, :] < cnt_rows[:, None]).astype(jnp.float32)
    inverse_count = 1.0 / cnt_rows.astype(jnp.float32)
    message = jax.nn.sigmoid(mixed_all[..., :channels]) * jax.nn.silu(mixed_all[..., channels:2 * channels]) * live_mask[..., None]
    summed = (lax.optimization_barrier(jnp.sum(message, axis=1)) * inverse_count[:, None]).astype(jnp.bfloat16)
    atom_next = h_rows + jnp.dot(summed, weight_atom, preferred_element_type=jnp.float32)
    paired = jnp.dot(bond_rows.reshape(row_count * slot_count, channels), weight_pair, preferred_element_type=jnp.float32).reshape(row_count, slot_count, 2 * channels)
    cosine_tile = cos_rows.reshape(row_count, slot_count, slot_count)
    angle_input = paired[:, :, None, :channels] + paired[:, None, :, channels:] + cosine_tile[..., None] * weight_cosine
    pair_mask = live_mask[:, :, None] * live_mask[:, None, :] * (1.0 - jnp.eye(slot_count, dtype=jnp.float32))
    angular = (lax.optimization_barrier(jnp.sum(jax.nn.silu(angle_input) * pair_mask[..., None], axis=2)) * inverse_count[:, None, None]).astype(jnp.bfloat16)
    update = jnp.dot(angular.reshape(row_count * slot_count, channels), weight_bond, preferred_element_type=jnp.float32).reshape(row_count, slot_count, channels)
    update = update * jax.nn.sigmoid(mixed_all[..., 2 * channels:]) * live_mask[..., None]
    bond_next = (bond_rows.astype(jnp.float32) + update).astype(jnp.bfloat16).reshape(row_count, slot_count * channels)
    return (atom_next, bond_next)

def reference(atom_features, bond_features, offsets, counts, cosines, weight_core, weight_atom, weight_pair, weight_cosine, weight_bond, weight_energy):
    total = atom_features.shape[0]
    block_rows = math.gcd(total, 1024)
    number = total // block_rows
    state = atom_features
    bonds_now = bond_features
    starts = jnp.arange(number, dtype=jnp.int32) * block_rows
    for layer_index in range(LAYERS):
        atom_table = state.astype(jnp.bfloat16)

        def block_step(items):
            block_start, h_rows, e_rows, off_rows, cnt_rows, cos_rows = items
            positions = block_start + jnp.arange(block_rows, dtype=jnp.int32)
            neighbour_ids = ((positions[:, None] + off_rows) % total).astype(jnp.int32)
            neighbours = jnp.take(atom_table, neighbour_ids, axis=0)
            return interact(h_rows, neighbours, e_rows, cnt_rows, cos_rows, weight_core[layer_index], weight_atom[layer_index], weight_pair[layer_index], weight_cosine[layer_index], weight_bond[layer_index])
        atom_next, bond_next = lax.map(block_step, (starts, state.reshape(number, block_rows, -1), bonds_now.reshape(number, block_rows, -1), offsets.reshape(number, block_rows, -1), counts.reshape(number, block_rows), cosines.reshape(number, block_rows, -1)))
        state = atom_next.reshape(total, -1)
        bonds_now = bond_next.reshape(total, -1)
    energy = jnp.sum(state * weight_energy) / math.sqrt(total)
    return (state, bonds_now, energy)
```

```python
import functools
import math

import jax
import jax.numpy as jnp
from jax import lax
from jax.experimental import pallas as pl
from jax.experimental.pallas import tpu as pltpu
from jax.sharding import PartitionSpec as P

C = 64
S = 16
BIG = 1e30
WIN = 17
f32 = jnp.float32
bf = jnp.bfloat16
MESH = pl.DeviceIdType.MESH


def angle_kernel(first, UNROLL, *refs):
    if first:
        b_ref, cos_ref, cnt_ref, wp_ref, wc_ref, bT_ref, cosT, ang_ref, PT, QT, wb = refs
    else:
        bT_ref, cosT, cnt_ref, wp_ref, wc_ref, ang_ref, PT, QT, wb = refs
    G = ang_ref.shape[1]
    CH = 32
    cnt = cnt_ref[...]
    inv = 1.0 / cnt.astype(f32)
    if first:
        for a in range(8):
            bT_ref[a * 128 : (a + 1) * 128, :] = b_ref[:, a * 128 : (a + 1) * 128].T
        for a in range(2):
            cosT[a * 128 : (a + 1) * 128, :] = cos_ref[:, a * 128 : (a + 1) * 128].T
    wb[...] = jnp.broadcast_to(wc_ref[...], (C, G)).astype(bf)
    wp = wp_ref[...]
    for j in range(S):
        pq = jnp.dot(wp, bT_ref[j * C : (j + 1) * C, :], preferred_element_type=f32)
        PT[j * C : (j + 1) * C, :] = pq[:C].astype(bf)
        QT[j * C : (j + 1) * C, :] = jnp.where(cnt > j, pq[C:], -BIG).astype(bf)

    def slot(j, carry):
        for cc in range(C // CH):
            rows = pl.ds(pl.multiple_of(j * C + cc * CH, CH), CH)
            p = PT[rows, :]
            total, part, n = None, None, 0
            for d in range(1, S):
                k = (j + d) % S
                cb = jnp.broadcast_to(cosT[pl.ds(j * S + k, 1), :], (CH, G)).astype(bf)
                q = QT[pl.ds(pl.multiple_of(k * C + cc * CH, CH), CH), :]
                h = p + q + cb * wb[cc * CH : (cc + 1) * CH, :]
                v = h + h * jnp.tanh(h)
                part = v if part is None else part + v
                n += 1
                if n % 4 == 0 or n == S - 1:
                    total = part if total is None else total + part
                    part = None
            ang_ref[rows, :] = (total.astype(f32) * inv).astype(bf)
        return carry

    lax.fori_loop(0, S, slot, 0, unroll=UNROLL)


def angles(first, b, cos, cnt, wpT, wc, G=256):
    N = cnt.shape[1]
    col = lambda r: pl.BlockSpec((r, G), lambda i: (0, i))
    full = lambda s: pl.BlockSpec(s, lambda i: (0, 0))
    sd = jax.ShapeDtypeStruct
    outs, shapes = [col(1024)], [sd((1024, N), bf)]
    if first:
        ins = [pl.BlockSpec((G, 1024), lambda i: (i, 0)), pl.BlockSpec((G, 256), lambda i: (i, 0))]
        outs = [col(1024), col(256)] + outs
        shapes = [sd((1024, N), bf), sd((256, N), f32)] + shapes
    else:
        ins = [col(1024), col(256)]
    return pl.pallas_call(
        functools.partial(angle_kernel, first, 4),
        grid=(N // G,),
        in_specs=ins + [col(1), full((128, C)), full((C, 1))],
        out_specs=outs,
        out_shape=shapes,
        scratch_shapes=[pltpu.VMEM((1024, G), bf), pltpu.VMEM((1024, G), bf), pltpu.VMEM((C, G), bf)],
        cost_estimate=pl.CostEstimate(flops=3 * 10**9, bytes_accessed=6 * 2**20, transcendentals=2**24),
        name="angles_first" if first else "angles_next",
    )(b, cos, cnt, wpT, wc)


def gate_kernel(last, t0, t1, t2, t3, t4, off_ref, cnt_ref, bT_ref, ang_ref, st_ref, wcT_ref, waT_ref, wbT_ref, *rest):
    if last:
        we_ref, ao_ref, bo_ref, en_ref, tall, cat, msg, bnew = rest
    else:
        so_ref, bnew, to_ref, tall, cat, msg = rest
    g = pl.program_id(0)
    G = bT_ref.shape[1]

    @pl.when(g == 0)
    def _():
        for n, t in enumerate((t0, t1, t2, t3, t4)):
            tall[n * 4 * C : (n + 1) * 4 * C, :] = t[...]

    cnt = cnt_ref[...]
    inv = 1.0 / cnt.astype(f32)
    cat[0:C, :] = st_ref[...].astype(bf)
    msg[...] = jnp.zeros_like(msg)
    base = lax.broadcasted_iota(jnp.int32, (1, G), 1) + 2048
    iota = lax.broadcasted_iota(jnp.int32, (256, G), 0).astype(f32).astype(bf)
    one, zero = jnp.ones((256, G), bf), jnp.zeros((256, G), bf)

    def slot(j, carry):
        rows = pl.ds(pl.multiple_of(j * C, C), C)
        idx = off_ref[pl.ds(j, 1), :] + base
        hi = idx >> 8
        lo = (idx & 255).astype(f32).astype(bf)
        hot = jnp.where(jnp.broadcast_to(lo, (256, G)) == iota, one, zero)
        res = jnp.dot(tall[pl.ds(pl.multiple_of(g * C, C), WIN * C), :], hot, preferred_element_type=f32)
        hib = jnp.broadcast_to(hi, (C, G))
        nb = res[:C]
        for h in range(1, WIN):
            nb = jnp.where(hib == h, res[h * C : (h + 1) * C], nb)
        cat[C : 2 * C, :] = nb.astype(bf)
        cat[2 * C :, :] = bT_ref[rows, :]
        mixed = jnp.dot(wcT_ref[...], cat[...], preferred_element_type=f32)
        gh, ch, bh = mixed[:C] * 0.5, mixed[C : 2 * C] * 0.5, mixed[2 * C :] * 0.5
        live = jnp.where(cnt > j, 0.5, 0.0)
        msg[...] += (jnp.tanh(gh) + 1.0) * (ch * (jnp.tanh(ch) + 1.0)) * live
        up = jnp.dot(wbT_ref[...], ang_ref[rows, :], preferred_element_type=f32)
        bnew[rows, :] = (bT_ref[rows, :].astype(f32) + up * ((jnp.tanh(bh) + 1.0) * live)).astype(bf)
        return carry

    lax.fori_loop(0, S, slot, 0)
    summed = (msg[...] * inv).astype(bf)
    st = st_ref[...] + jnp.dot(waT_ref[...], summed, preferred_element_type=f32)
    if last:
        for h in range(G // 128):
            ao_ref[h * 128 : (h + 1) * 128, :] = st[:, h * 128 : (h + 1) * 128].T
            for a in range(8):
                bo_ref[h * 128 : (h + 1) * 128, a * 128 : (a + 1) * 128] = bnew[
                    a * 128 : (a + 1) * 128, h * 128 : (h + 1) * 128
                ].T
        en_ref[...] = jnp.sum(st * we_ref[...], axis=0, keepdims=True)
    else:
        so_ref[...] = st
        to_ref[...] = st.astype(bf)


def gate(last, tables, offT, cnt, bT, ang, st, wcT, waT, wbT, we=None, G=256):
    N = bT.shape[1]
    full = lambda s: pl.BlockSpec(s, lambda i: (0, 0))
    col = lambda r: pl.BlockSpec((r, G), lambda i: (0, i))
    sd = jax.ShapeDtypeStruct
    ins = [full((256, 256))] * 5 + [col(S), col(1), col(1024), col(1024), col(C)]
    ins += [full((192, 192)), full((C, C)), full((C, C))]
    args = [*tables, offT, cnt, bT, ang, st, wcT, waT, wbT]
    scratch = [pltpu.VMEM((20 * C, 256), bf), pltpu.VMEM((192, G), bf), pltpu.VMEM((C, G), f32)]
    if last:
        ins.append(full((C, 1)))
        args.append(we)
        outs = [pl.BlockSpec((G, C), lambda i: (i, 0)), pl.BlockSpec((G, 1024), lambda i: (i, 0)), col(1)]
        shapes = [sd((N, C), f32), sd((N, 1024), bf), sd((1, N), f32)]
        scratch.append(pltpu.VMEM((1024, G), bf))
    else:
        outs = [col(C), col(1024), pl.BlockSpec((C, G), lambda i: (i, 0))]
        shapes = [sd((C, N), f32), sd((1024, N), bf), sd((N // G * C, G), bf)]
    return pl.pallas_call(
        functools.partial(gate_kernel, last),
        grid=(N // G,),
        in_specs=ins,
        out_specs=outs,
        out_shape=shapes,
        scratch_shapes=scratch,
        name="gate_last" if last else "gate_mid",
    )(*args)


def total_kernel(e_ref, o_ref, near, part, far, s_near, r_near, s_far, r_far):
    space, rep = lax.axis_index("space"), lax.axis_index("rep")
    chip, core = space // 2, space % 2
    close, away = [], []
    for dc in range(2):
        for dr in range(4):
            if dc or dr:
                close.append((chip * 2 + (core + dc) % 2, (rep + dr) % 4))
    for d in range(1, 16):
        away.append((((chip + d) % 16) * 2 + core, rep))
    barrier = pltpu.get_barrier_semaphore()
    for to in close + away:
        pl.semaphore_signal(barrier, inc=1, device_id=to, device_id_type=MESH)
    pl.semaphore_wait(barrier, len(close) + len(away))

    def spread(src, slots, mine, targets, ssem, rsem):
        copies = []
        for n, to in enumerate(targets):
            copies.append(
                pltpu.make_async_remote_copy(
                    src_ref=src,
                    dst_ref=slots.at[mine],
                    send_sem=ssem.at[n],
                    recv_sem=rsem.at[n],
                    device_id=to,
                    device_id_type=MESH,
                )
            )
            copies[-1].start()
        return copies

    me = core * 4 + rep
    near[me] = e_ref[...]
    for c in spread(e_ref, near, me, close, s_near, r_near):
        c.wait()
    acc = near[0]
    for n in range(1, 8):
        acc = acc + near[n]
    part[...] = acc
    far[chip] = acc
    for c in spread(part, far, chip, away, s_far, r_far):
        c.wait()
    acc = far[0]
    for n in range(1, 16):
        acc = acc + far[n]
    o_ref[...] = jnp.full((8, 128), jnp.sum(acc), f32)


def total(e):
    return pl.pallas_call(
        total_kernel,
        out_shape=jax.ShapeDtypeStruct((8, 128), f32),
        in_specs=[pl.BlockSpec(memory_space=pltpu.VMEM)],
        out_specs=pl.BlockSpec(memory_space=pltpu.VMEM),
        scratch_shapes=[
            pltpu.VMEM((8, 8, 128), f32),
            pltpu.VMEM((8, 128), f32),
            pltpu.VMEM((16, 8, 128), f32),
            pltpu.SemaphoreType.DMA((7,)),
            pltpu.SemaphoreType.DMA((7,)),
            pltpu.SemaphoreType.DMA((15,)),
            pltpu.SemaphoreType.DMA((15,)),
        ],
        compiler_params=pltpu.CompilerParams(collective_id=0, has_side_effects=True),
        name="total",
    )(e)[0, 0]


def around(block):
    count = lax.axis_size("space") * lax.axis_size("rep")
    out = []
    for d in (-2, -1, 0, 1, 2):
        if d == 0:
            out.append(block)
        else:
            out.append(lax.ppermute(block, ("space", "rep"), [((i + d) % count, i) for i in range(count)]))
    return out


def per_device(atoms, bonds, offsets, counts, cosines, w_core, w_atom, w_pair, w_cos, w_bond, w_energy):
    quarter = bonds.shape[0]
    own = lax.dynamic_slice_in_dim(atoms, lax.axis_index("rep") * quarter, quarter, 0)
    st = own.T
    block = st.astype(bf).reshape(C, 4, 256).transpose(1, 0, 2).reshape(256, 256)
    cnt = counts.reshape(1, quarter)
    offT = offsets.T
    wcT = w_core.transpose(0, 2, 1)
    waT = w_atom.transpose(0, 2, 1)
    wbT = w_bond.transpose(0, 2, 1)
    wpT = w_pair.transpose(0, 2, 1) * jnp.asarray(0.5, bf)
    wc = 0.5 * w_cos[:, :, None]
    tables = around(block)
    bT, cosT, ang = angles(True, bonds, cosines, cnt, wpT[0], wc[0])
    st, bT, block = gate(False, tables, offT, cnt, bT, ang, st, wcT[0], waT[0], wbT[0])
    tables = around(block)
    (ang,) = angles(False, bT, cosT, cnt, wpT[1], wc[1])
    ao, bo, en = gate(True, tables, offT, cnt, bT, ang, st, wcT[1], waT[1], wbT[1], w_energy[:, None])
    energy = total(en.reshape(8, 128)) / math.sqrt(lax.axis_size("space") * atoms.shape[0])
    return ao, bo, energy


def solution(mesh):
    both = ("space", "rep")
    return jax.shard_map(
        per_device,
        mesh=mesh,
        in_specs=(P("space", None), P(both, None), P(both, None), P(both), P(both, None)) + (P(),) * 6,
        out_specs=(P(both, None), P(both, None), P()),
        check_vma=False,
    )
```

```python
import functools
import math

import jax
import jax.numpy as jnp
from jax import lax
from jax.experimental import pallas as pl
from jax.experimental.pallas import tpu as pltpu
from jax.sharding import PartitionSpec as P

C = 64
S = 16
BIG = 1e30
WIN = 17
f32 = jnp.float32
bf = jnp.bfloat16
MESH = pl.DeviceIdType.MESH


def swap(ref, pad):
    rows, cols = ref.shape
    full = jnp.pad(ref[...].astype(f32), ((0, pad - rows), (0, pad - cols))) if (rows, cols) != (pad, pad) else ref[...]
    out = jnp.concatenate(
        [
            jnp.concatenate(
                [full[b * 128 : (b + 1) * 128, a * 128 : (a + 1) * 128].T for b in range(pad // 128)], axis=1
            )
            for a in range(pad // 128)
        ],
        axis=0,
    )
    return out[:cols, :rows]


def column(row, width):
    return jnp.broadcast_to(row, (width, C)).T


def angle_kernel(layer, *refs):
    if layer == 0:
        b_ref, cos_ref, at_ref, cnt_ref, wp_ref, wc_ref, bT_ref, cosT, ang_ref, tab_ref = refs[:10]
    else:
        bT_ref, cosT, at_ref, cnt_ref, wp_ref, wc_ref, ang_ref, tab_ref = refs[:8]
    PT, QT, wb, CB, wpT, tabs, ssem, rsem = refs[-8:]
    G = ang_ref.shape[1]
    g = pl.program_id(0)
    space, rep = lax.axis_index("space"), lax.axis_index("rep")
    spaces, reps = lax.axis_size("space"), lax.axis_size("rep")
    copies = []
    for n, d in enumerate((1, -1, 2, -2)):
        to = (space * reps + rep + d + spaces * reps) % (spaces * reps)
        src = tabs.at[2]
        copies.append(
            pltpu.make_async_remote_copy(
                src_ref=src,
                dst_ref=tabs.at[2 - d],
                send_sem=ssem.at[n],
                recv_sem=rsem.at[n],
                device_id=(to // reps, to % reps),
                device_id_type=MESH,
            )
        )

    @pl.when(g == 0)
    def _():
        if layer == 0:
            for n in range(4):
                piece = at_ref[:, pl.ds(pl.multiple_of(rep * 4 * G + n * G, G), G)]
                tabs[2, n * C : (n + 1) * C, :] = piece.astype(bf)
        else:
            tabs[2] = at_ref[...]
        wpT[...] = (swap(wp_ref, 128)[:, :C] * 0.5).astype(bf)
        wb[...] = (column(wc_ref[layer : layer + 1, :], G) * 0.5).astype(bf).reshape(8, 8, G)
        barrier = pltpu.get_barrier_semaphore()
        for d in (1, -1, 2, -2):
            to = (space * reps + rep + d + spaces * reps) % (spaces * reps)
            pl.semaphore_signal(barrier, inc=1, device_id=(to // reps, to % reps), device_id_type=MESH)
        pl.semaphore_wait(barrier, 4)
        for c in copies:
            c.start()

    cnt = cnt_ref[...]
    inv = 1.0 / cnt.astype(f32)
    if layer == 0:
        for a in range(8):
            bT_ref[a * 128 : (a + 1) * 128, :] = b_ref[:, a * 128 : (a + 1) * 128].T
        for a in range(2):
            cosT[a * 128 : (a + 1) * 128, :] = cos_ref[:, a * 128 : (a + 1) * 128].T
    wp = wpT[...]
    for j in range(S):
        pq = jnp.dot(wp, bT_ref[j * C : (j + 1) * C, :], preferred_element_type=f32)
        PT[j] = pq[:C].astype(bf).reshape(8, 8, G)
        QT[j] = jnp.where(cnt > j, pq[C:], -BIG).astype(bf).reshape(8, 8, G)
    for r in range(S * S):
        if r % (S + 1):
            CB[r] = jnp.broadcast_to(cosT[r : r + 1, :], (8, G)).astype(bf)

    def slot(j, carry):
        p, w = PT[j], wb[...]
        total, part, n = None, None, 0
        for d in range(1, S):
            k = (j + d) % S
            h = p + QT[k] + CB[j * S + k][None] * w
            v = h + h * jnp.tanh(h)
            part = v if part is None else part + v
            n += 1
            if n % 4 == 0 or n == S - 1:
                total = part if total is None else total + part
                part = None
        rows = pl.ds(pl.multiple_of(j * C, C), C)
        ang_ref[rows, :] = (total.reshape(C, G).astype(f32) * inv).astype(bf)
        return carry

    lax.fori_loop(0, S, slot, 0, unroll=2)

    @pl.when(g == pl.num_programs(0) - 1)
    def _():
        for c in copies:
            c.wait()
        for n in range(5):
            tab_ref[n * 4 * C : (n + 1) * 4 * C, :] = tabs[n]


def angles(layer, b, cos, at, cnt, wp, wc, G=256):
    N = cnt.shape[1]
    col = lambda r: pl.BlockSpec((r, G), lambda i: (0, i))
    full = lambda s: pl.BlockSpec(s, lambda i: (0, 0))
    sd = jax.ShapeDtypeStruct
    outs, shapes = [col(1024), full((20 * C, G))], [sd((1024, N), bf), sd((20 * C, G), bf)]
    if layer == 0:
        ins = [pl.BlockSpec((G, 1024), lambda i: (i, 0)), pl.BlockSpec((G, 256), lambda i: (i, 0))]
        outs = [col(1024), col(256)] + outs
        shapes = [sd((1024, N), bf), sd((256, N), f32)] + shapes
    else:
        ins = [col(1024), col(256)]
    return pl.pallas_call(
        functools.partial(angle_kernel, layer),
        grid=(N // G,),
        in_specs=ins + [full(at.shape), col(1), pl.BlockSpec((None, C, 2 * C), lambda i: (layer, 0, 0)), full((2, C))],
        out_specs=outs,
        out_shape=shapes,
        scratch_shapes=[
            pltpu.VMEM((S, 8, 8, G), bf),
            pltpu.VMEM((S, 8, 8, G), bf),
            pltpu.VMEM((8, 8, G), bf),
            pltpu.VMEM((S * S, 8, G), bf),
            pltpu.VMEM((2 * C, C), bf),
            pltpu.VMEM((5, 4 * C, G), bf),
            pltpu.SemaphoreType.DMA((4,)),
            pltpu.SemaphoreType.DMA((4,)),
        ],
        compiler_params=pltpu.CompilerParams(collective_id=1 + layer, has_side_effects=True),
        name=f"angles_{layer}",
    )(b, cos, at, cnt, wp, wc)


def gate_kernel(layer, last, tall, off_ref, cnt_ref, bT_ref, ang_ref, st_ref, wc_ref, wa_ref, wb_ref, *rest):
    if last:
        we_ref, so_ref, bo_ref, en_ref, msg, wcT_ref, waT_ref, wbT_ref, bnew, we = rest
    else:
        so_ref, bnew, to_ref, msg, wcT_ref, waT_ref, wbT_ref = rest
    g = pl.program_id(0)
    G = bT_ref.shape[1]

    @pl.when(g == 0)
    def _():
        wcT_ref[...] = (swap(wc_ref, 256) * 0.5).astype(bf)
        waT_ref[...] = swap(wa_ref, 128).astype(bf)
        wbT_ref[...] = swap(wb_ref, 128).astype(bf)
        if last:
            we[...] = column(we_ref[...], G)

    cnt = cnt_ref[...]
    inv = 1.0 / cnt.astype(f32)
    if layer == 0:
        state = st_ref[:, pl.ds(pl.multiple_of(lax.axis_index("rep") * 4 * G + g * G, G), G)]
    else:
        state = st_ref[...]
    ctr = state.astype(bf)
    msg[...] = jnp.zeros_like(msg)
    base = lax.broadcasted_iota(jnp.int32, (1, G), 1) + 2048
    iota = lax.broadcasted_iota(jnp.int32, (256, G), 0).astype(f32).astype(bf)
    one, zero = jnp.ones((256, G), bf), jnp.zeros((256, G), bf)

    def fetch(j):
        idx = off_ref[pl.ds(j, 1), :] + base
        hi = idx >> 8
        lo = (idx & 255).astype(f32).astype(bf)
        hot = jnp.where(jnp.broadcast_to(lo, (256, G)) == iota, one, zero)
        res = jnp.dot(tall[pl.ds(pl.multiple_of(g * C, C), WIN * C), :], hot, preferred_element_type=f32)
        hib = jnp.broadcast_to(hi, (C, G))
        nb = res[:C]
        for h in range(1, WIN):
            nb = jnp.where(hib == h, res[h * C : (h + 1) * C], nb)
        return nb.astype(bf)

    def finish(j, nb):
        rows = pl.ds(pl.multiple_of(j * C, C), C)
        own = bT_ref[rows, :]
        mixed = jnp.dot(wcT_ref[...], jnp.concatenate([ctr, nb, own], axis=0), preferred_element_type=f32)
        live = jnp.broadcast_to(jnp.where(cnt > j, 0.5, 0.0), (C, G))
        up = jnp.dot(wbT_ref[...], ang_ref[rows, :], preferred_element_type=f32)
        gh, ch, bh = mixed[:C], mixed[C : 2 * C], mixed[2 * C :]
        gl = jnp.tanh(gh) * live + live
        msg[...] += gl * (ch * jnp.tanh(ch) + ch)
        gate = jnp.tanh(bh) * live + live
        bnew[rows, :] = (own.astype(f32) + up * gate).astype(bf)

    def slot(j, nb):
        nxt = fetch(jnp.minimum(j + 1, S - 1))
        finish(j, nb)
        return nxt

    lax.fori_loop(0, S, slot, fetch(0), unroll=8)
    summed = (msg[...] * inv).astype(bf)
    st = state + jnp.dot(waT_ref[...], summed, preferred_element_type=f32)
    so_ref[...] = st
    if last:
        for h in range(G // 128):
            for a in range(8):
                bo_ref[h * 128 : (h + 1) * 128, a * 128 : (a + 1) * 128] = bnew[
                    a * 128 : (a + 1) * 128, h * 128 : (h + 1) * 128
                ].T
        en_ref[...] = jnp.sum(st * we[...], axis=0, keepdims=True)
    else:
        to_ref[...] = st.astype(bf)


def gate(layer, last, table, offT, cnt, bT, ang, st, wc, wa, wb, we, G=256):
    N = bT.shape[1]
    full = lambda s: pl.BlockSpec(s, lambda i: (0, 0))
    col = lambda r: pl.BlockSpec((r, G), lambda i: (0, i))
    of = lambda r, c: pl.BlockSpec((None, r, c), lambda i: (layer, 0, 0))
    sd = jax.ShapeDtypeStruct
    ins = [full((20 * C, G)), col(S), col(1), col(1024), col(1024), full(st.shape) if layer == 0 else col(C)]
    ins += [of(3 * C, 3 * C), of(C, C), of(C, C)]
    args = [table, offT, cnt, bT, ang, st, wc, wa, wb]
    scratch = [pltpu.VMEM((C, G), f32), pltpu.VMEM((3 * C, 3 * C), bf), pltpu.VMEM((C, C), bf), pltpu.VMEM((C, C), bf)]
    if last:
        ins.append(full((1, C)))
        args.append(we)
        outs = [col(C), pl.BlockSpec((G, 1024), lambda i: (i, 0)), col(1)]
        shapes = [sd((C, N), f32), sd((N, 1024), bf), sd((1, N), f32)]
        scratch += [pltpu.VMEM((1024, G), bf), pltpu.VMEM((C, G), f32)]
    else:
        outs = [col(C), col(1024), pl.BlockSpec((C, G), lambda i: (i, 0))]
        shapes = [sd((C, N), f32), sd((1024, N), bf), sd((N // G * C, G), bf)]
    return pl.pallas_call(
        functools.partial(gate_kernel, layer, last),
        grid=(N // G,),
        in_specs=ins,
        out_specs=outs,
        out_shape=shapes,
        scratch_shapes=scratch,
        name=f"gate_{layer}",
    )(*args)


def total_kernel(e_ref, o_ref, near, part, far, s_near, r_near, s_far, r_far):
    space, rep = lax.axis_index("space"), lax.axis_index("rep")
    chip, core = space // 2, space % 2
    close, away = [], []
    for dc in range(2):
        for dr in range(4):
            if dc or dr:
                close.append((chip * 2 + (core + dc) % 2, (rep + dr) % 4))
    for d in range(1, 16):
        away.append((((chip + d) % 16) * 2 + core, rep))
    barrier = pltpu.get_barrier_semaphore()
    for to in close + away:
        pl.semaphore_signal(barrier, inc=1, device_id=to, device_id_type=MESH)
    pl.semaphore_wait(barrier, len(close) + len(away))

    def spread(src, slots, mine, targets, ssem, rsem):
        copies = []
        for n, to in enumerate(targets):
            copies.append(
                pltpu.make_async_remote_copy(
                    src_ref=src,
                    dst_ref=slots.at[mine],
                    send_sem=ssem.at[n],
                    recv_sem=rsem.at[n],
                    device_id=to,
                    device_id_type=MESH,
                )
            )
            copies[-1].start()
        return copies

    me = core * 4 + rep
    near[me] = e_ref[...]
    for c in spread(e_ref, near, me, close, s_near, r_near):
        c.wait()
    acc = near[0]
    for n in range(1, 8):
        acc = acc + near[n]
    part[...] = acc
    far[chip] = acc
    for c in spread(part, far, chip, away, s_far, r_far):
        c.wait()
    acc = far[0]
    for n in range(1, 16):
        acc = acc + far[n]
    o_ref[...] = jnp.full((8, 128), jnp.sum(acc), f32)


def total(e):
    return pl.pallas_call(
        total_kernel,
        out_shape=jax.ShapeDtypeStruct((8, 128), f32),
        in_specs=[pl.BlockSpec(memory_space=pltpu.VMEM)],
        out_specs=pl.BlockSpec(memory_space=pltpu.VMEM),
        scratch_shapes=[
            pltpu.VMEM((8, 8, 128), f32),
            pltpu.VMEM((8, 128), f32),
            pltpu.VMEM((16, 8, 128), f32),
            pltpu.SemaphoreType.DMA((7,)),
            pltpu.SemaphoreType.DMA((7,)),
            pltpu.SemaphoreType.DMA((15,)),
            pltpu.SemaphoreType.DMA((15,)),
        ],
        compiler_params=pltpu.CompilerParams(collective_id=0, has_side_effects=True),
        name="total",
    )(e)[0, 0]


def per_device(atoms, bonds, offsets, counts, cosines, w_core, w_atom, w_pair, w_cos, w_bond, w_energy):
    cnt = counts.reshape(1, -1)
    offT = offsets.T
    st = atoms.T
    we = w_energy.reshape(1, -1)
    bT, cosT, ang, table = angles(0, bonds, cosines, st, cnt, w_pair, w_cos)
    st, bT, block = gate(0, False, table, offT, cnt, bT, ang, st, w_core, w_atom, w_bond, we)
    ang, table = angles(1, bT, cosT, block, cnt, w_pair, w_cos)
    st, bo, en = gate(1, True, table, offT, cnt, bT, ang, st, w_core, w_atom, w_bond, we)
    energy = total(en.reshape(8, 128)) / math.sqrt(lax.axis_size("space") * atoms.shape[0])
    return st.T, bo, energy


def solution(mesh):
    both = ("space", "rep")
    return jax.shard_map(
        per_device,
        mesh=mesh,
        in_specs=(P("space", None), P(both, None), P(both, None), P(both), P(both, None)) + (P(),) * 6,
        out_specs=(P(both, None), P(both, None), P()),
        check_vma=False,
    )
```

```python
import functools
import math

import jax
import jax.numpy as jnp
from jax import lax
from jax.experimental import pallas as pl
from jax.experimental.pallas import tpu as pltpu
from jax.sharding import PartitionSpec as P

C = 64
S = 16
BIG = 1e30
WIN = 17
f32 = jnp.float32
bf = jnp.bfloat16
MESH = pl.DeviceIdType.MESH


def swap(ref, pad):
    rows, cols = ref.shape
    full = jnp.pad(ref[...].astype(f32), ((0, pad - rows), (0, pad - cols))) if (rows, cols) != (pad, pad) else ref[...]
    out = jnp.concatenate(
        [
            jnp.concatenate(
                [full[b * 128 : (b + 1) * 128, a * 128 : (a + 1) * 128].T for b in range(pad // 128)], axis=1
            )
            for a in range(pad // 128)
        ],
        axis=0,
    )
    return out[:cols, :rows]


def column(row, width):
    return jnp.broadcast_to(row, (width, C)).T


def pairs(bT, wp, cnt, cosT, PT, QT, CB):
    G = cnt.shape[1]
    for j in range(S):
        pq = jnp.dot(wp, bT[j * C : (j + 1) * C, :], preferred_element_type=f32)
        PT[j] = pq[:C].astype(bf).reshape(8, 8, G)
        QT[j] = jnp.where(cnt > j, pq[C:], -BIG).astype(bf).reshape(8, 8, G)
    for r in range(S * S):
        if r % (S + 1):
            CB[r] = jnp.broadcast_to(cosT[r : r + 1, :], (8, G)).astype(bf)


def sums(PT, QT, CB, wb, inv, ang_ref):
    G = inv.shape[1]

    def slot(j, carry):
        p, w = PT[j], wb[...]
        total, part, n = None, None, 0
        for d in range(1, S):
            k = (j + d) % S
            h = p + QT[k] + CB[j * S + k][None] * w
            v = h + h * jnp.tanh(h)
            part = v if part is None else part + v
            n += 1
            if n % 4 == 0 or n == S - 1:
                total = part if total is None else total + part
                part = None
        rows = pl.ds(pl.multiple_of(j * C, C), C)
        ang_ref[rows, :] = (total.reshape(C, G).astype(f32) * inv).astype(bf)
        return carry

    lax.fori_loop(0, S, slot, 0, unroll=2)


def pair_scratch(G):
    return [
        pltpu.VMEM((S, 8, 8, G), bf),
        pltpu.VMEM((S, 8, 8, G), bf),
        pltpu.VMEM((8, 8, G), bf),
        pltpu.VMEM((S * S, 8, G), bf),
        pltpu.VMEM((2 * C, C), bf),
    ]


def pair_weights(wp_ref, wc_ref, layer, wpT, wb):
    G = wb.shape[2]
    wpT[...] = (swap(wp_ref, 128)[:, :C] * 0.5).astype(bf)
    wb[...] = (column(wc_ref[layer : layer + 1, :], G) * 0.5).astype(bf).reshape(8, 8, G)


AROUND = (1, -1, 2, -2)


def beside(d):
    spaces, reps = lax.axis_size("space"), lax.axis_size("rep")
    to = (lax.axis_index("space") * reps + lax.axis_index("rep") + d + spaces * reps) % (spaces * reps)
    return (to // reps, to % reps)


def send(src, dst, ssem, rsem, to):
    return pltpu.make_async_remote_copy(
        src_ref=src, dst_ref=dst, send_sem=ssem, recv_sem=rsem, device_id=to, device_id_type=MESH
    )


def first_kernel(b_ref, cos_ref, at_ref, cnt_ref, wp_ref, wc_ref, bT_ref, cosT, ang_ref, tab_ref, *scratch):
    PT, QT, wb, CB, wpT, tabs, ssem, rsem = scratch
    G = ang_ref.shape[1]
    g = pl.program_id(0)
    copies = [send(tabs.at[2], tabs.at[2 - d], ssem.at[n], rsem.at[n], beside(d)) for n, d in enumerate(AROUND)]

    @pl.when(g == 0)
    def _():
        barrier = pltpu.get_barrier_semaphore()
        for d in AROUND:
            pl.semaphore_signal(barrier, inc=1, device_id=beside(d), device_id_type=MESH)
        rep = lax.axis_index("rep")
        for n in range(4):
            piece = at_ref[:, pl.ds(pl.multiple_of(rep * 4 * G + n * G, G), G)]
            tabs[2, n * C : (n + 1) * C, :] = piece.astype(bf)
        pair_weights(wp_ref, wc_ref, 0, wpT, wb)
        pl.semaphore_wait(barrier, 4)
        for c in copies:
            c.start()

    cnt = cnt_ref[...]
    for a in range(8):
        bT_ref[a * 128 : (a + 1) * 128, :] = b_ref[:, a * 128 : (a + 1) * 128].T
    for a in range(2):
        cosT[a * 128 : (a + 1) * 128, :] = cos_ref[:, a * 128 : (a + 1) * 128].T
    pairs(bT_ref, wpT[...], cnt, cosT, PT, QT, CB)
    sums(PT, QT, CB, wb, 1.0 / cnt.astype(f32), ang_ref)

    @pl.when(g == pl.num_programs(0) - 1)
    def _():
        for c in copies:
            c.wait()
        for n in range(5):
            tab_ref[n * 4 * C : (n + 1) * 4 * C, :] = tabs[n]


def full(*s):
    return pl.BlockSpec(s, lambda i: (0,) * len(s))


def first(b, cos, at, cnt, wp, wc, G=256):
    N = cnt.shape[1]
    col = lambda r: pl.BlockSpec((r, G), lambda i: (0, i))
    sd = jax.ShapeDtypeStruct
    return pl.pallas_call(
        first_kernel,
        grid=(N // G,),
        in_specs=[
            pl.BlockSpec((G, 1024), lambda i: (i, 0)),
            pl.BlockSpec((G, 256), lambda i: (i, 0)),
            full(*at.shape),
            col(1),
            pl.BlockSpec((None, C, 2 * C), lambda i: (0, 0, 0)),
            full(2, C),
        ],
        out_specs=[col(1024), col(256), col(1024), full(20 * C, G)],
        out_shape=[sd((1024, N), bf), sd((256, N), f32), sd((1024, N), bf), sd((20 * C, G), bf)],
        scratch_shapes=pair_scratch(G)
        + [pltpu.VMEM((5, 4 * C, G), bf), pltpu.SemaphoreType.DMA((4,)), pltpu.SemaphoreType.DMA((4,))],
        compiler_params=pltpu.CompilerParams(collective_id=0, has_side_effects=True),
        name="first",
    )(b, cos, at, cnt, wp, wc)


def peers():
    space, rep = lax.axis_index("space"), lax.axis_index("rep")
    chip, core = space // 2, space % 2
    chips, reps = lax.axis_size("space") // 2, lax.axis_size("rep")
    close = []
    for dc in range(2):
        for dr in range(reps):
            if dc or dr:
                close.append((chip * 2 + (core + dc) % 2, (rep + dr) % reps))
    away = [(((chip + d) % chips) * 2 + core, rep) for d in range(1, chips)]
    return close, away, core * reps + rep, chip


def gate_kernel(last, tall, off_ref, cnt_ref, bT_ref, cosT, st_ref, wc_ref, wa_ref, wp_ref, wcos_ref, *rest):
    if last:
        we_ref, so_ref, gt_ref, ang_ref, en_ref = rest[:5]
        msg, wcT_ref, waT_ref, PT, QT, wb, CB, wpT = rest[5:13]
        we, mine, near, part, far, s_near, r_near, s_far, r_far = rest[13:]
        close, away, seat, chip = peers()
        greet = close + away
        hop1 = [send(mine, near.at[seat], s_near.at[n], r_near.at[n], to) for n, to in enumerate(close)]
        hop2 = [send(part, far.at[chip], s_far.at[n], r_far.at[n], to) for n, to in enumerate(away)]
    else:
        wbond_ref, old_ref, so_ref, bo_ref, ang_ref, tab_ref = rest[:6]
        msg, wcT_ref, waT_ref, PT, QT, wb, CB, wpT = rest[6:14]
        wbT_ref, keep, tabs, ssem, rsem = rest[14:]
        greet = [beside(d) for d in AROUND]
    i = pl.program_id(0)
    G = cnt_ref.shape[1]
    barrier = pltpu.get_barrier_semaphore()

    def moves(g):
        part_of = pl.ds(pl.multiple_of(g * C, C), C)
        return [
            send(tabs.at[2, part_of], tabs.at[2 - d, part_of], ssem.at[n, g], rsem.at[n, g], beside(d))
            for n, d in enumerate(AROUND)
        ]

    @pl.when(i == 0)
    def _():
        for to in greet:
            pl.semaphore_signal(barrier, inc=1, device_id=to, device_id_type=MESH)
        wcT_ref[...] = (swap(wc_ref, 256) * 0.5).astype(bf)
        waT_ref[...] = swap(wa_ref, 128).astype(bf)
        pair_weights(wp_ref, wcos_ref, 1, wpT, wb)
        if last:
            we[...] = column(we_ref[...], G)
            mine[...] = jnp.zeros_like(mine)
        else:
            wbT_ref[...] = swap(wbond_ref, 128).astype(bf)

    if not last:

        @pl.when(i == 1)
        def _():
            pl.semaphore_wait(barrier, len(greet))

        @pl.when((i >= 1) & (i <= 4))
        def _():
            for c in moves(i - 1):
                c.start()

    cnt = cnt_ref[...]
    inv = 1.0 / cnt.astype(f32)

    @pl.when(i < 4)
    def _():
        if last:
            state = st_ref[...]
        else:
            state = st_ref[:, pl.ds(pl.multiple_of(lax.axis_index("rep") * 4 * G + i * G, G), G)]
        ctr = state.astype(bf)
        msg[...] = jnp.zeros_like(msg)
        base = lax.broadcasted_iota(jnp.int32, (1, G), 1) + 2048
        iota = lax.broadcasted_iota(jnp.int32, (256, G), 0).astype(f32).astype(bf)
        one, zero = jnp.ones((256, G), bf), jnp.zeros((256, G), bf)

        def fetch(j):
            idx = off_ref[pl.ds(j, 1), :] + base
            hi = idx >> 8
            lo = (idx & 255).astype(f32).astype(bf)
            hot = jnp.where(jnp.broadcast_to(lo, (256, G)) == iota, one, zero)
            res = jnp.dot(tall[pl.ds(pl.multiple_of(i * C, C), WIN * C), :], hot, preferred_element_type=f32)
            hib = jnp.broadcast_to(hi, (C, G))
            nb = res[:C]
            for h in range(1, WIN):
                nb = jnp.where(hib == h, res[h * C : (h + 1) * C], nb)
            return nb.astype(bf)

        def finish(j, nb):
            rows = pl.ds(pl.multiple_of(j * C, C), C)
            own = bT_ref[rows, :]
            mixed = jnp.dot(wcT_ref[...], jnp.concatenate([ctr, nb, own], axis=0), preferred_element_type=f32)
            live = jnp.broadcast_to(jnp.where(cnt > j, 0.5, 0.0), (C, G))
            gh, ch, bh = mixed[:C], mixed[C : 2 * C], mixed[2 * C :]
            gl = jnp.tanh(gh) * live + live
            msg[...] += gl * (ch * jnp.tanh(ch) + ch)
            gate = jnp.tanh(bh) * live + live
            if last:
                gt_ref[rows, :] = gate.astype(bf)
            else:
                up = jnp.dot(wbT_ref[...], old_ref[rows, :], preferred_element_type=f32)
                bo_ref[rows, :] = (own.astype(f32) + up * gate).astype(bf)

        def slot(j, nb):
            nxt = fetch(jnp.minimum(j + 1, S - 1))
            finish(j, nb)
            return nxt

        lax.fori_loop(0, S, slot, fetch(0), unroll=8)
        summed = (msg[...] * inv).astype(bf)
        st = state + jnp.dot(waT_ref[...], summed, preferred_element_type=f32)
        so_ref[...] = st
        if last:
            e = jnp.sum((st * we[...]).reshape(8, 8, G), axis=0)
            mine[...] += e[:, :128] + e[:, 128:]
        else:
            tabs[2, pl.ds(pl.multiple_of(i * C, C), C), :] = st.astype(bf)

    if not last:

        @pl.when(i < 2)
        def _():
            keep[i] = bo_ref[...]

    if last:

        @pl.when(i == 4)
        def _():
            pl.semaphore_wait(barrier, len(greet))
            for c in hop1:
                c.start()
            near[seat] = mine[...]

        @pl.when(i == 5)
        def _():
            for c in hop1:
                c.wait()
            acc = near[0]
            for n in range(1, near.shape[0]):
                acc = acc + near[n]
            part[...] = acc
            far[chip] = acc
            for c in hop2:
                c.start()

    @pl.when(i >= 4)
    def _():
        pairs(bT_ref if last else keep.at[i - 4], wpT[...], cnt, cosT, PT, QT, CB)
        sums(PT, QT, CB, wb, inv, ang_ref)

    @pl.when(i == 5)
    def _():
        if last:
            for c in hop2:
                c.wait()
            acc = far[0]
            for n in range(1, far.shape[0]):
                acc = acc + far[n]
            scale = 1.0 / math.sqrt(lax.axis_size("space") * lax.axis_size("rep") * 4 * G)
            en_ref[0, 0] = jnp.sum(acc) * scale
        else:
            for g in range(4):
                for c in moves(g):
                    c.wait()
            for n in range(5):
                tab_ref[n * 4 * C : (n + 1) * 4 * C, :] = tabs[n]


def gate(last, table, offT, cnt, bT, cosT, st, w_core, w_atom, w_pair, w_cos, extra, G=256):
    N = bT.shape[1]
    layer = 1 if last else 0
    back = 2 if last else 4
    now = lambda r: pl.BlockSpec((r, G), lambda i: (0, i - back * (i // 4)))
    hold = lambda r: pl.BlockSpec((r, G), lambda i: (0, i - (i // 4) * (i - 3)))
    late = lambda r, at: pl.BlockSpec((r, G), lambda i: (0, at + i // 5))
    of = lambda l, r, c: pl.BlockSpec((None, r, c), lambda i: (l, 0, 0))
    sd = jax.ShapeDtypeStruct
    ins = [full(20 * C, G), now(S), now(1), now(1024) if last else hold(1024), late(256, 2 if last else 0)]
    ins += [hold(C) if last else full(*st.shape), of(layer, 3 * C, 3 * C), of(layer, C, C), of(1, C, 2 * C), full(2, C)]
    scratch = [pltpu.VMEM((C, G), f32), pltpu.VMEM((3 * C, 3 * C), bf), pltpu.VMEM((C, C), bf)] + pair_scratch(G)
    dma = pltpu.SemaphoreType.DMA
    if last:
        ins += [full(1, C)]
        outs = [hold(C), hold(1024), late(1024, 0), pl.BlockSpec(memory_space=pltpu.SMEM)]
        shapes = [sd((C, N), f32), sd((1024, N), bf), sd((1024, N // 2), bf), sd((1, 1), f32)]
        tile = pltpu.VMEM((8, 128), f32)
        chips = lax.axis_size("space") // 2
        seats = 2 * lax.axis_size("rep")
        scratch += [pltpu.VMEM((C, G), f32), tile, pltpu.VMEM((seats, 8, 128), f32), tile]
        scratch += [pltpu.VMEM((chips, 8, 128), f32), dma((seats - 1,)), dma((seats - 1,)), dma((chips - 1,)), dma((chips - 1,))]
    else:
        ins += [of(0, C, C), hold(1024)]
        outs = [hold(C), hold(1024), late(1024, 0), full(20 * C, G)]
        shapes = [sd((C, N), f32), sd((1024, N), bf), sd((1024, N // 2), bf), sd((20 * C, G), bf)]
        scratch += [pltpu.VMEM((C, C), bf), pltpu.VMEM((2, 1024, G), bf), pltpu.VMEM((5, 4 * C, G), bf), dma((4, 4)), dma((4, 4))]
    return pl.pallas_call(
        functools.partial(gate_kernel, last),
        grid=(6,),
        in_specs=ins,
        out_specs=outs,
        out_shape=shapes,
        scratch_shapes=scratch,
        compiler_params=pltpu.CompilerParams(collective_id=1 + layer, has_side_effects=True),
        name=f"gate_{layer}",
    )(table, offT, cnt, bT, cosT, st, w_core, w_atom, w_pair, w_cos, *extra)


def bond_kernel(bT_ref, early, later, gt_ref, st_ref, wb_ref, so_ref, bo_ref, wbT, bnew):
    i = pl.program_id(0)
    G = bT_ref.shape[1]

    @pl.when(i == 0)
    def _():
        wbT[...] = swap(wb_ref, 128).astype(bf)

    so_ref[...] = st_ref[...]

    def update(ang):
        for j in range(S):
            rows = slice(j * C, (j + 1) * C)
            up = jnp.dot(wbT[...], ang[rows, :], preferred_element_type=f32)
            new = bT_ref[rows, :].astype(f32) + up * gt_ref[rows, :].astype(f32)
            bnew[rows, :] = new.astype(bf)

    @pl.when(i < 2)
    def _():
        update(early)

    @pl.when(i >= 2)
    def _():
        update(later)

    for h in range(G // 128):
        for a in range(8):
            cut = bnew[a * 128 : (a + 1) * 128, h * 128 : (h + 1) * 128]
            bo_ref[h * 128 : (h + 1) * 128, a * 128 : (a + 1) * 128] = cut.T


def bond(bT, early, later, gates, st, w_bond, G=256):
    N = bT.shape[1]
    col = lambda r: pl.BlockSpec((r, G), lambda i: (0, i))
    sd = jax.ShapeDtypeStruct
    return pl.pallas_call(
        bond_kernel,
        grid=(N // G,),
        in_specs=[
            col(1024),
            pl.BlockSpec((1024, G), lambda i: (0, jnp.minimum(i, 1))),
            pl.BlockSpec((1024, G), lambda i: (0, jnp.maximum(i - 2, 0))),
            col(1024),
            col(C),
            pl.BlockSpec((None, C, C), lambda i: (1, 0, 0)),
        ],
        out_specs=[col(C), pl.BlockSpec((G, 1024), lambda i: (i, 0))],
        out_shape=[sd((C, N), f32), sd((N, 1024), bf)],
        scratch_shapes=[pltpu.VMEM((C, C), bf), pltpu.VMEM((1024, G), bf)],
        name="bond",
    )(bT, early, later, gates, st, w_bond)


def per_device(atoms, bonds, offsets, counts, cosines, w_core, w_atom, w_pair, w_cos, w_bond, w_energy):
    cnt = counts.reshape(1, -1)
    offT = offsets.T
    st = atoms.T
    shared = (w_core, w_atom, w_pair, w_cos)
    bT, cosT, old, table = first(bonds, cosines, st, cnt, w_pair, w_cos)
    st, bT, early, table = gate(False, table, offT, cnt, bT, cosT, st, *shared, (w_bond, old))
    st, gates, later, energy = gate(True, table, offT, cnt, bT, cosT, st, *shared, (w_energy.reshape(1, -1),))
    st, bo = bond(bT, early, later, gates, st, w_bond)
    return st.T, bo, energy.reshape(())


def solution(mesh):
    both = ("space", "rep")
    return jax.shard_map(
        per_device,
        mesh=mesh,
        in_specs=(P("space", None), P(both, None), P(both, None), P(both), P(both, None)) + (P(),) * 6,
        out_specs=(P(both, None), P(both, None), P()),
        check_vma=False,
    )
```

```python
import functools
import math

import jax
import jax.numpy as jnp
from jax import lax
from jax.experimental import pallas as pl
from jax.experimental.pallas import tpu as pltpu
from jax.sharding import PartitionSpec as P

C = 64
S = 16
BIG = 1e30
WIN = 17
f32 = jnp.float32
bf = jnp.bfloat16
MESH = pl.DeviceIdType.MESH


def swap(ref, pad):
    rows, cols = ref.shape
    full = jnp.pad(ref[...].astype(f32), ((0, pad - rows), (0, pad - cols))) if (rows, cols) != (pad, pad) else ref[...]
    out = jnp.concatenate(
        [
            jnp.concatenate(
                [full[b * 128 : (b + 1) * 128, a * 128 : (a + 1) * 128].T for b in range(pad // 128)], axis=1
            )
            for a in range(pad // 128)
        ],
        axis=0,
    )
    return out[:cols, :rows]


def column(row, width):
    return jnp.broadcast_to(row, (width, C)).T


def pairs(bT, wp, cnt, cosT, PT, QT, CB):
    G = cnt.shape[1]
    for j in range(S):
        pq = jnp.dot(wp, bT[j * C : (j + 1) * C, :], preferred_element_type=f32)
        PT[j] = pq[:C].astype(bf).reshape(8, 8, G)
        QT[j] = jnp.where(cnt > j, pq[C:], -BIG).astype(bf).reshape(8, 8, G)
    for r in range(S * S):
        if r % (S + 1):
            CB[r] = jnp.broadcast_to(cosT[r : r + 1, :], (8, G)).astype(bf)


def angle_slot(j, PT, QT, CB, w, inv, ang_ref):
    G = inv.shape[1]
    p = PT[j]
    total, part, n = None, None, 0
    for d in range(1, S):
        k = (j + d) % S
        h = p + QT[k] + CB[j * S + k][None] * w
        v = h + h * jnp.tanh(h)
        part = v if part is None else part + v
        n += 1
        if n % 4 == 0 or n == S - 1:
            total = part if total is None else total + part
            part = None
    rows = pl.ds(pl.multiple_of(j * C, C), C)
    ang_ref[rows, :] = (total.reshape(C, G).astype(f32) * inv).astype(bf)


def sums(PT, QT, CB, wb, inv, ang_ref):
    def slot(j, carry):
        angle_slot(j, PT, QT, CB, wb[...], inv, ang_ref)
        return carry

    lax.fori_loop(0, S, slot, 0, unroll=2)


def pair_scratch(G):
    return [
        pltpu.VMEM((S, 8, 8, G), bf),
        pltpu.VMEM((S, 8, 8, G), bf),
        pltpu.VMEM((8, 8, G), bf),
        pltpu.VMEM((S * S, 8, G), bf),
        pltpu.VMEM((2 * C, C), bf),
    ]


def pair_weights(wp_ref, wc_ref, layer, wpT, wb):
    G = wb.shape[2]
    wpT[...] = (swap(wp_ref, 128)[:, :C] * 0.5).astype(bf)
    wb[...] = (column(wc_ref[layer : layer + 1, :], G) * 0.5).astype(bf).reshape(8, 8, G)


AROUND = (1, -1, 2, -2)


def beside(d):
    spaces, reps = lax.axis_size("space"), lax.axis_size("rep")
    to = (lax.axis_index("space") * reps + lax.axis_index("rep") + d + spaces * reps) % (spaces * reps)
    return (to // reps, to % reps)


def send(src, dst, ssem, rsem, to):
    return pltpu.make_async_remote_copy(
        src_ref=src, dst_ref=dst, send_sem=ssem, recv_sem=rsem, device_id=to, device_id_type=MESH
    )


def first_kernel(b_ref, cos_ref, at_ref, cnt_ref, wp_ref, wc_ref, bT_ref, cosT, ang_ref, tab_ref, st_ref, *scratch):
    PT, QT, wb, CB, wpT, tabs, ssem, rsem, own, osem = scratch
    G = ang_ref.shape[1]
    g = pl.program_id(0)
    copies = [send(tabs.at[2], tabs.at[2 - d], ssem.at[n], rsem.at[n], beside(d)) for n, d in enumerate(AROUND)]
    barrier = pltpu.get_barrier_semaphore()
    cols = pl.ds(pl.multiple_of(lax.axis_index("rep") * 4 * G, 4 * G), 4 * G)
    fill = pltpu.make_async_copy(at_ref.at[:, cols], own, osem)

    @pl.when(g == 0)
    def _():
        fill.start()
        for d in AROUND:
            pl.semaphore_signal(barrier, inc=1, device_id=beside(d), device_id_type=MESH)
        pair_weights(wp_ref, wc_ref, 0, wpT, wb)

    @pl.when(g == 1)
    def _():
        fill.wait()
        for n in range(4):
            piece = own[:, n * G : (n + 1) * G]
            st_ref[n] = piece
            tabs[2, n * C : (n + 1) * C, :] = piece.astype(bf)

    @pl.when(g == 2)
    def _():
        pl.semaphore_wait(barrier, 4)
        for c in copies:
            c.start()

    for a in range(8):
        bT_ref[a * 128 : (a + 1) * 128, :] = b_ref[:, a * 128 : (a + 1) * 128].T
    for a in range(2):
        cosT[a * 128 : (a + 1) * 128, :] = cos_ref[:, a * 128 : (a + 1) * 128].T

    @pl.when(g >= 2)
    def _():
        cnt = cnt_ref[...]
        pairs(bT_ref, wpT[...], cnt, cosT, PT, QT, CB)
        sums(PT, QT, CB, wb, 1.0 / cnt.astype(f32), ang_ref)

    @pl.when(g == 3)
    def _():
        for c in copies:
            c.wait()
        for n in range(5):
            tab_ref[n * 4 * C : (n + 1) * 4 * C, :] = tabs[n]


def full(*s):
    return pl.BlockSpec(s, lambda i: (0,) * len(s))


def seg(r, at, G=256):
    return pl.BlockSpec((None, r, G), lambda i: (at(i), 0, 0))


def row(r, at, G=256):
    return pl.BlockSpec((r, G), lambda i: (0, at(i)))


def first(b, cos, at, cnt, wp, wc, G=256):
    turn = lambda i: (i + 2) % 4
    sd = jax.ShapeDtypeStruct
    return pl.pallas_call(
        first_kernel,
        grid=(4,),
        in_specs=[
            pl.BlockSpec((G, 1024), lambda i: (turn(i), 0)),
            pl.BlockSpec((G, 256), lambda i: (turn(i), 0)),
            pl.BlockSpec(memory_space=pl.ANY),
            row(1, turn),
            pl.BlockSpec((None, C, 2 * C), lambda i: (0, 0, 0)),
            full(2, C),
        ],
        out_specs=[seg(1024, turn), seg(256, turn), seg(1024, lambda i: i // 3), full(20 * C, G), full(4, C, G)],
        out_shape=[
            sd((4, 1024, G), bf),
            sd((4, 256, G), f32),
            sd((2, 1024, G), bf),
            sd((20 * C, G), bf),
            sd((4, C, G), f32),
        ],
        scratch_shapes=pair_scratch(G)
        + [pltpu.VMEM((5, 4 * C, G), bf), pltpu.SemaphoreType.DMA((4,)), pltpu.SemaphoreType.DMA((4,))]
        + [pltpu.VMEM((C, 4 * G), f32), pltpu.SemaphoreType.DMA],
        compiler_params=pltpu.CompilerParams(collective_id=0, has_side_effects=True),
        name="first",
    )(b, cos, at, cnt, wp, wc)


def peers():
    space, rep = lax.axis_index("space"), lax.axis_index("rep")
    chip, core = space // 2, space % 2
    chips, reps = lax.axis_size("space") // 2, lax.axis_size("rep")
    close = []
    for dc in range(2):
        for dr in range(reps):
            if dc or dr:
                close.append((chip * 2 + (core + dc) % 2, (rep + dr) % reps))
    away = [(((chip + d) % chips) * 2 + core, rep) for d in range(1, chips)]
    return close, away, core * reps + rep, chip


def gate_kernel(last, tall, off_ref, cnt_ref, bT_ref, cosT, st_ref, wc_ref, wa_ref, wp_ref, wcos_ref, *rest):
    if last:
        we_ref, so_ref, gt_ref, ang_ref, en_ref = rest[:5]
        msg, wcT_ref, waT_ref, PT, QT, wb, CB, wpT = rest[5:13]
        we, mine, near, part, far, s_near, r_near, s_far, r_far = rest[13:]
        close, away, seat, chip = peers()
        greet = close + away
        hop1 = [send(mine, near.at[seat], s_near.at[n], r_near.at[n], to) for n, to in enumerate(close)]
        hop2 = [send(part, far.at[chip], s_far.at[n], r_far.at[n], to) for n, to in enumerate(away)]
    else:
        wbond_ref, old_ref, b2_ref, cnt2_ref, so_ref, bo_ref, ang_ref, tab_ref = rest[:8]
        msg, wcT_ref, waT_ref, PT, QT, wb, CB, wpT = rest[8:16]
        wbT_ref, olds, keep, tabs, ssem, rsem = rest[16:]
        greet = [beside(d) for d in AROUND]
    i = pl.program_id(0)
    G = cnt_ref.shape[1]
    layer = 1 if last else 0
    barrier = pltpu.get_barrier_semaphore()

    def moves(g):
        part_of = pl.ds(pl.multiple_of(g * C, C), C)
        return [
            send(tabs.at[2, part_of], tabs.at[2 - d, part_of], ssem.at[n, g], rsem.at[n, g], beside(d))
            for n, d in enumerate(AROUND)
        ]

    @pl.when(i == 0)
    def _():
        for to in greet:
            pl.semaphore_signal(barrier, inc=1, device_id=to, device_id_type=MESH)
        wcT_ref[...] = (swap(wc_ref, 256) * 0.5).astype(bf)
        waT_ref[...] = swap(wa_ref, 128).astype(bf)
        pair_weights(wp_ref.at[layer], wcos_ref, layer, wpT, wb)
        if last:
            we[...] = column(we_ref[...], G)
            mine[...] = jnp.zeros_like(mine)
        else:
            wbT_ref[...] = swap(wbond_ref, 128).astype(bf)

    if not last:

        @pl.when(i == 1)
        def _():
            pl.semaphore_wait(barrier, len(greet))

        @pl.when((i >= 1) & (i <= 4))
        def _():
            for c in moves(i - 1):
                c.start()

    cnt = cnt_ref[...]
    inv = 1.0 / cnt.astype(f32)

    if not last:

        @pl.when(i < 2)
        def _():
            olds[i] = old_ref[...]
            pairs(b2_ref, wpT[...], cnt2_ref[...], cosT, PT, QT, CB)

        @pl.when(i == 4)
        def _():
            pair_weights(wp_ref.at[1], wcos_ref, 1, wpT, wb)

    @pl.when(i < 4)
    def _():
        state = st_ref[...]
        ctr = state.astype(bf)
        msg[...] = jnp.zeros_like(msg)
        base = lax.broadcasted_iota(jnp.int32, (1, G), 1) + 2048
        iota = lax.broadcasted_iota(jnp.int32, (256, G), 0).astype(f32).astype(bf)
        one, zero = jnp.ones((256, G), bf), jnp.zeros((256, G), bf)

        def fetch(j):
            idx = off_ref[pl.ds(j, 1), :] + base
            hi = idx >> 8
            lo = (idx & 255).astype(f32).astype(bf)
            hot = jnp.where(jnp.broadcast_to(lo, (256, G)) == iota, one, zero)
            res = jnp.dot(tall[pl.ds(pl.multiple_of(i * C, C), WIN * C), :], hot, preferred_element_type=f32)
            hib = jnp.broadcast_to(hi, (C, G))
            nb = res[:C]
            for h in range(1, WIN):
                nb = jnp.where(hib == h, res[h * C : (h + 1) * C], nb)
            return nb.astype(bf)

        def finish(j, nb):
            rows = pl.ds(pl.multiple_of(j * C, C), C)
            own = bT_ref[rows, :]
            mixed = jnp.dot(wcT_ref[...], jnp.concatenate([ctr, nb, own], axis=0), preferred_element_type=f32)
            live = jnp.broadcast_to(jnp.where(cnt > j, 0.5, 0.0), (C, G))
            gh, ch, bh = mixed[:C], mixed[C : 2 * C], mixed[2 * C :]
            gl = jnp.tanh(gh) * live + live
            msg[...] += gl * (ch * jnp.tanh(ch) + ch)
            gate = jnp.tanh(bh) * live + live
            if last:
                gt_ref[rows, :] = gate.astype(bf)
            else:
                up = jnp.dot(wbT_ref[...], olds[i, rows, :], preferred_element_type=f32)
                bo_ref[rows, :] = (own.astype(f32) + up * gate).astype(bf)

        def slot(j, nb):
            nxt = fetch(jnp.minimum(j + 1, S - 1))
            finish(j, nb)
            return nxt

        def both(j, nb):
            nxt = fetch(jnp.minimum(j + 1, S - 1))
            finish(j, nb)
            angle_slot(j, PT, QT, CB, wb[...], inv2, olds.at[i + 2])
            return nxt

        if last:
            lax.fori_loop(0, S, slot, fetch(0), unroll=8)
        else:
            inv2 = 1.0 / cnt2_ref[...].astype(f32)

            @pl.when(i < 2)
            def _():
                lax.fori_loop(0, S, both, fetch(0), unroll=8)

            @pl.when(i >= 2)
            def _():
                lax.fori_loop(0, S, slot, fetch(0), unroll=8)

        summed = (msg[...] * inv).astype(bf)
        st = state + jnp.dot(waT_ref[...], summed, preferred_element_type=f32)
        so_ref[...] = st
        if last:
            e = jnp.sum((st * we[...]).reshape(8, 8, G), axis=0)
            mine[...] += e[:, :128] + e[:, 128:]
        else:
            tabs[2, pl.ds(pl.multiple_of(i * C, C), C), :] = st.astype(bf)

    if not last:

        @pl.when(i < 2)
        def _():
            keep[i] = bo_ref[...]

    if last:

        @pl.when(i == 4)
        def _():
            pl.semaphore_wait(barrier, len(greet))
            for c in hop1:
                c.start()
            near[seat] = mine[...]

        @pl.when(i == 5)
        def _():
            for c in hop1:
                c.wait()
            acc = near[0]
            for n in range(1, near.shape[0]):
                acc = acc + near[n]
            part[...] = acc
            far[chip] = acc
            for c in hop2:
                c.start()

    @pl.when(i >= 4)
    def _():
        pairs(bT_ref if last else keep.at[i - 4], wpT[...], cnt, cosT, PT, QT, CB)
        sums(PT, QT, CB, wb, inv, ang_ref)

    @pl.when(i == 5)
    def _():
        if last:
            for c in hop2:
                c.wait()
            acc = far[0]
            for n in range(1, far.shape[0]):
                acc = acc + far[n]
            scale = 1.0 / math.sqrt(lax.axis_size("space") * lax.axis_size("rep") * 4 * G)
            en_ref[0, 0] = jnp.sum(acc) * scale
        else:
            for g in range(4):
                for c in moves(g):
                    c.wait()
            for n in range(5):
                tab_ref[n * 4 * C : (n + 1) * 4 * C, :] = tabs[n]


def gate(last, table, offT, cnt, bT, cosT, st, w_core, w_atom, w_pair, w_cos, extra, G=256):
    layer = 1 if last else 0
    back = 2 if last else 4
    now = lambda i: i - back * (i // 4)
    hold = lambda i: i - (i // 4) * (i - 3)
    late = lambda i: i // 5
    ahead = lambda i: jnp.minimum(2 + i, 3)
    turns = lambda i: (i // 4) * (i - 4) + (1 - i // 4) * ahead(i)
    of = lambda l, r, c: pl.BlockSpec((None, r, c), lambda i: (l, 0, 0))
    sd = jax.ShapeDtypeStruct
    ins = [full(20 * C, G), row(S, hold), row(1, now), seg(1024, now if last else hold)]
    ins += [seg(256, (lambda i: 2 + i // 5) if last else turns), seg(C, hold)]
    ins += [of(layer, 3 * C, 3 * C), of(layer, C, C), full(2, C, 2 * C), full(2, C)]
    scratch = [pltpu.VMEM((C, G), f32), pltpu.VMEM((3 * C, 3 * C), bf), pltpu.VMEM((C, C), bf)] + pair_scratch(G)
    dma = pltpu.SemaphoreType.DMA
    if last:
        ins += [full(1, C)]
        outs = [seg(C, hold), seg(1024, hold), seg(1024, late), pl.BlockSpec(memory_space=pltpu.SMEM)]
        shapes = [sd((4, C, G), f32), sd((4, 1024, G), bf), sd((2, 1024, G), bf), sd((1, 1), f32)]
        tile = pltpu.VMEM((8, 128), f32)
        chips = lax.axis_size("space") // 2
        seats = 2 * lax.axis_size("rep")
        scratch += [pltpu.VMEM((C, G), f32), tile, pltpu.VMEM((seats, 8, 128), f32), tile]
        scratch += [pltpu.VMEM((chips, 8, 128), f32), dma((seats - 1,)), dma((seats - 1,)), dma((chips - 1,)), dma((chips - 1,))]
    else:
        ins += [of(0, C, C), seg(1024, lambda i: jnp.minimum(i, 1)), seg(1024, ahead), row(1, ahead)]
        outs = [seg(C, hold), seg(1024, hold), seg(1024, late), full(20 * C, G)]
        shapes = [sd((4, C, G), f32), sd((4, 1024, G), bf), sd((2, 1024, G), bf), sd((20 * C, G), bf)]
        scratch += [pltpu.VMEM((C, C), bf), pltpu.VMEM((4, 1024, G), bf), pltpu.VMEM((2, 1024, G), bf), pltpu.VMEM((5, 4 * C, G), bf), dma((4, 4)), dma((4, 4))]
    return pl.pallas_call(
        functools.partial(gate_kernel, last),
        grid=(6,),
        in_specs=ins,
        out_specs=outs,
        out_shape=shapes,
        scratch_shapes=scratch,
        compiler_params=pltpu.CompilerParams(collective_id=1 + layer, has_side_effects=True),
        name=f"gate_{layer}",
    )(table, offT, cnt, bT, cosT, st, w_core, w_atom, w_pair, w_cos, *extra)


def bond_kernel(bT_ref, early, later, gt_ref, st_ref, wb_ref, so_ref, bo_ref, wbT, bnew):
    i = pl.program_id(0)
    G = bT_ref.shape[1]

    @pl.when(i == 0)
    def _():
        wbT[...] = swap(wb_ref, 128).astype(bf)

    so_ref[...] = st_ref[...]

    def update(ang):
        for j in range(S):
            rows = slice(j * C, (j + 1) * C)
            up = jnp.dot(wbT[...], ang[rows, :], preferred_element_type=f32)
            new = bT_ref[rows, :].astype(f32) + up * gt_ref[rows, :].astype(f32)
            bnew[rows, :] = new.astype(bf)

    @pl.when(i < 2)
    def _():
        update(early)

    @pl.when(i >= 2)
    def _():
        update(later)

    for h in range(G // 128):
        for a in range(8):
            cut = bnew[a * 128 : (a + 1) * 128, h * 128 : (h + 1) * 128]
            bo_ref[h * 128 : (h + 1) * 128, a * 128 : (a + 1) * 128] = cut.T


def bond(bT, early, later, gates, st, w_bond, G=256):
    step = lambda i: i
    sd = jax.ShapeDtypeStruct
    return pl.pallas_call(
        bond_kernel,
        grid=(4,),
        in_specs=[
            seg(1024, step),
            seg(1024, lambda i: jnp.minimum(i, 1)),
            seg(1024, lambda i: jnp.maximum(i - 2, 0)),
            seg(1024, step),
            seg(C, step),
            pl.BlockSpec((None, C, C), lambda i: (1, 0, 0)),
        ],
        out_specs=[row(C, step), pl.BlockSpec((G, 1024), lambda i: (i, 0))],
        out_shape=[sd((C, 4 * G), f32), sd((4 * G, 1024), bf)],
        scratch_shapes=[pltpu.VMEM((C, C), bf), pltpu.VMEM((1024, G), bf)],
        name="bond",
    )(bT, early, later, gates, st, w_bond)


def per_device(atoms, bonds, offsets, counts, cosines, w_core, w_atom, w_pair, w_cos, w_bond, w_energy):
    cnt = counts.reshape(1, -1)
    offT = offsets.T
    shared = (w_core, w_atom, w_pair, w_cos)
    bT, cosT, old, table, st = first(bonds, cosines, atoms.T, cnt, w_pair, w_cos)
    st, bT, early, table = gate(False, table, offT, cnt, bT, cosT, st, *shared, (w_bond, old, bT, cnt))
    st, gates, later, energy = gate(True, table, offT, cnt, bT, cosT, st, *shared, (w_energy.reshape(1, -1),))
    st, bo = bond(bT, early, later, gates, st, w_bond)
    return st.T, bo, energy.reshape(())


def solution(mesh):
    both = ("space", "rep")
    return jax.shard_map(
        per_device,
        mesh=mesh,
        in_specs=(P("space", None), P(both, None), P(both, None), P(both), P(both, None)) + (P(),) * 6,
        out_specs=(P(both, None), P(both, None), P()),
        check_vma=False,
    )
```

```python
import functools
import math

import jax
import jax.numpy as jnp
from jax import lax
from jax.experimental import pallas as pl
from jax.experimental.pallas import tpu as pltpu
from jax.sharding import PartitionSpec as P

C = 64
S = 16
BIG = 1e30
WIN = 17
f32 = jnp.float32
bf = jnp.bfloat16
MESH = pl.DeviceIdType.MESH


def swap(ref, pad):
    rows, cols = ref.shape
    full = jnp.pad(ref[...].astype(f32), ((0, pad - rows), (0, pad - cols))) if (rows, cols) != (pad, pad) else ref[...]
    out = jnp.concatenate(
        [
            jnp.concatenate(
                [full[b * 128 : (b + 1) * 128, a * 128 : (a + 1) * 128].T for b in range(pad // 128)], axis=1
            )
            for a in range(pad // 128)
        ],
        axis=0,
    )
    return out[:cols, :rows]


def column(row, width):
    return jnp.broadcast_to(row, (width, C)).T


def pairs(bT, wp, cnt, cosT, PT, QT, CB):
    G = cnt.shape[1]
    for j in range(S):
        pq = jnp.dot(wp, bT[j * C : (j + 1) * C, :], preferred_element_type=f32)
        PT[j] = pq[:C].astype(bf).reshape(8, 8, G)
        QT[j] = jnp.where(cnt > j, pq[C:], -BIG).astype(bf).reshape(8, 8, G)
    for r in range(S * S):
        if r % (S + 1):
            CB[r] = jnp.broadcast_to(cosT[r : r + 1, :], (8, G)).astype(bf)


def angle_slot(j, PT, QT, CB, w, inv, ang_ref):
    G = inv.shape[1]
    p = PT[j]
    total, part, n = None, None, 0
    for d in range(1, S):
        k = (j + d) % S
        h = p + QT[k] + CB[j * S + k][None] * w
        v = h + h * jnp.tanh(h)
        part = v if part is None else part + v
        n += 1
        if n % 4 == 0 or n == S - 1:
            total = part if total is None else total + part
            part = None
    rows = pl.ds(pl.multiple_of(j * C, C), C)
    ang_ref[rows, :] = (total.reshape(C, G).astype(f32) * inv).astype(bf)


def sums(PT, QT, CB, wb, inv, ang_ref):
    def slot(j, carry):
        angle_slot(j, PT, QT, CB, wb[...], inv, ang_ref)
        return carry

    lax.fori_loop(0, S, slot, 0, unroll=2)


def pair_scratch(G):
    return [
        pltpu.VMEM((S, 8, 8, G), bf),
        pltpu.VMEM((S, 8, 8, G), bf),
        pltpu.VMEM((8, 8, G), bf),
        pltpu.VMEM((S * S, 8, G), bf),
        pltpu.VMEM((2 * C, C), bf),
    ]


def pair_weights(wp_ref, wc_ref, layer, wpT, wb):
    G = wb.shape[2]
    wpT[...] = (swap(wp_ref, 128)[:, :C] * 0.5).astype(bf)
    wb[...] = (column(wc_ref[layer : layer + 1, :], G) * 0.5).astype(bf).reshape(8, 8, G)


AROUND = (1, -1, 2, -2)


def beside(d):
    spaces, reps = lax.axis_size("space"), lax.axis_size("rep")
    to = (lax.axis_index("space") * reps + lax.axis_index("rep") + d + spaces * reps) % (spaces * reps)
    return (to // reps, to % reps)


def send(src, dst, ssem, rsem, to):
    return pltpu.make_async_remote_copy(
        src_ref=src, dst_ref=dst, send_sem=ssem, recv_sem=rsem, device_id=to, device_id_type=MESH
    )


def first_kernel(b_ref, cos_ref, at_ref, cnt_ref, wp_ref, wc_ref, bT_ref, cosT, ang_ref, tab_ref, st_ref, *scratch):
    PT, QT, wb, CB, wpT, tabs, out, ssem, rsem, own, osem = scratch
    G = ang_ref.shape[1]
    g = pl.program_id(0)
    spaces = lax.axis_size("space")
    space, rep = lax.axis_index("space"), lax.axis_index("rep")
    down = rep // 2
    ahead = ((space + 1 - 2 * down + spaces) % spaces, rep)
    behind = ((space - 1 + 2 * down + spaces) % spaces, rep)
    near = send(out.at[0], tabs.at[down * (4 - rep // 3)], ssem.at[0], rsem.at[0], ahead)
    far = send(out.at[1], tabs.at[1 + 3 * down], ssem.at[1], rsem.at[1], ahead)
    ends = rep % 3 == 0
    barrier = pltpu.get_barrier_semaphore()
    fill = pltpu.make_async_copy(at_ref, own, osem)

    def block(which, dst):
        for n in range(4):
            piece = own[:, pl.ds(pl.multiple_of((which * 4 + n) * G, G), G)]
            dst[n * C : (n + 1) * C, :] = piece.astype(bf)

    @pl.when(g == 0)
    def _():
        fill.start()
        pl.semaphore_signal(barrier, inc=1, device_id=behind, device_id_type=MESH)
        pair_weights(wp_ref, wc_ref, 0, wpT, wb)

    @pl.when(g == 1)
    def _():
        fill.wait()
        block((1 - down) * (2 + rep), out.at[0])
        block(3 - 2 * down, out.at[1])
        for m in range(5):
            mine = rep - 2 + m

            @pl.when((mine >= 0) & (mine <= 3))
            def _():
                block(mine, tab_ref.at[pl.ds(m * 4 * C, 4 * C)])

        for n in range(4):
            st_ref[n] = own[:, pl.ds(pl.multiple_of((rep * 4 + n) * G, G), G)]

    @pl.when(g == 2)
    def _():
        pl.semaphore_wait(barrier, 1)
        near.start()

        @pl.when(ends)
        def _():
            far.start()

    for a in range(8):
        bT_ref[a * 128 : (a + 1) * 128, :] = b_ref[:, a * 128 : (a + 1) * 128].T
    for a in range(2):
        cosT[a * 128 : (a + 1) * 128, :] = cos_ref[:, a * 128 : (a + 1) * 128].T

    @pl.when(g == 3)
    def _():
        cnt = cnt_ref[...]
        pairs(bT_ref, wpT[...], cnt, cosT, PT, QT, CB)
        sums(PT, QT, CB, wb, 1.0 / cnt.astype(f32), ang_ref)
        near.wait()

        @pl.when(ends)
        def _():
            far.wait()

        for m in range(5):
            mine = rep - 2 + m

            @pl.when((mine < 0) | (mine > 3))
            def _():
                tab_ref[m * 4 * C : (m + 1) * 4 * C, :] = tabs[m]


def full(*s):
    return pl.BlockSpec(s, lambda i: (0,) * len(s))


def seg(r, at, G=256):
    return pl.BlockSpec((None, r, G), lambda i: (at(i), 0, 0))


def row(r, at, G=256):
    return pl.BlockSpec((r, G), lambda i: (0, at(i)))


def first(b, cos, at, cnt, wp, wc, G=256):
    turn = lambda i: (i + 1) % 4
    sd = jax.ShapeDtypeStruct
    return pl.pallas_call(
        first_kernel,
        grid=(4,),
        in_specs=[
            pl.BlockSpec((G, 1024), lambda i: (turn(i), 0)),
            pl.BlockSpec((G, 256), lambda i: (turn(i), 0)),
            pl.BlockSpec(memory_space=pl.ANY),
            row(1, turn),
            pl.BlockSpec((None, C, 2 * C), lambda i: (0, 0, 0)),
            full(2, C),
        ],
        out_specs=[seg(1024, turn), seg(256, turn), full(1024, G), full(20 * C, G), full(4, C, G)],
        out_shape=[
            sd((4, 1024, G), bf),
            sd((4, 256, G), f32),
            sd((1024, G), bf),
            sd((20 * C, G), bf),
            sd((4, C, G), f32),
        ],
        scratch_shapes=pair_scratch(G)
        + [pltpu.VMEM((5, 4 * C, G), bf), pltpu.VMEM((2, 4 * C, G), bf)]
        + [pltpu.SemaphoreType.DMA((2,)), pltpu.SemaphoreType.DMA((2,)), pltpu.VMEM(at.shape, f32), pltpu.SemaphoreType.DMA],
        compiler_params=pltpu.CompilerParams(collective_id=0, has_side_effects=True),
        name="first",
    )(b, cos, at, cnt, wp, wc)


def peers():
    space, rep = lax.axis_index("space"), lax.axis_index("rep")
    chip, core = space // 2, space % 2
    chips, reps = lax.axis_size("space") // 2, lax.axis_size("rep")
    close = []
    for dc in range(2):
        for dr in range(reps):
            if dc or dr:
                close.append((chip * 2 + (core + dc) % 2, (rep + dr) % reps))
    away = [(((chip + d) % chips) * 2 + core, rep) for d in range(1, chips)]
    return close, away, core * reps + rep, chip


def gate_kernel(last, tall, off_ref, cnt_ref, bT_ref, cosT, st_ref, wc_ref, wa_ref, wp_ref, wcos_ref, *rest):
    if last:
        wbond_ref, we_ref, old_ref, so_ref, bo_ref, en_ref = rest[:6]
        msg, wcT_ref, waT_ref, PT, QT, wb, CB, wpT, wbT_ref = rest[6:15]
        we, gts, angs, mine, near, part, far, s_near, r_near, s_far, r_far = rest[15:]
        close, away, seat, chip = peers()
        greet = close + away
        hop1 = [send(mine, near.at[seat], s_near.at[n], r_near.at[n], to) for n, to in enumerate(close)]
        hop2 = [send(part, far.at[chip], s_far.at[n], r_far.at[n], to) for n, to in enumerate(away)]
    else:
        wbond_ref, old_ref, b2_ref, cnt2_ref, so_ref, bo_ref, ang_ref, tab_ref = rest[:8]
        msg, wcT_ref, waT_ref, PT, QT, wb, CB, wpT, wbT_ref = rest[8:17]
        olds, keep, tabs, ssem, rsem = rest[17:]
        greet = [beside(d) for d in AROUND]
    i = pl.program_id(0)
    G = cnt_ref.shape[1]
    layer = 1 if last else 0
    barrier = pltpu.get_barrier_semaphore()

    def moves(g):
        part_of = pl.ds(pl.multiple_of(g * C, C), C)
        return [
            send(tabs.at[2, part_of], tabs.at[2 - d, part_of], ssem.at[n, g], rsem.at[n, g], beside(d))
            for n, d in enumerate(AROUND)
        ]

    @pl.when(i == 0)
    def _():
        for to in greet:
            pl.semaphore_signal(barrier, inc=1, device_id=to, device_id_type=MESH)
        wcT_ref[...] = (swap(wc_ref, 256) * 0.5).astype(bf)
        waT_ref[...] = swap(wa_ref, 128).astype(bf)
        pair_weights(wp_ref.at[layer], wcos_ref, layer, wpT, wb)
        if last:
            we[...] = column(we_ref[...], G)
            mine[...] = jnp.zeros_like(mine)
        else:
            olds[0] = old_ref[...]
        wbT_ref[...] = swap(wbond_ref, 128).astype(bf)

    if not last:

        @pl.when(i == 1)
        def _():
            pl.semaphore_wait(barrier, len(greet))

        @pl.when((i >= 1) & (i <= 4))
        def _():
            for c in moves(i - 1):
                c.start()

    cnt = cnt_ref[...]
    inv = 1.0 / cnt.astype(f32)

    if not last:

        cnt2 = cnt2_ref[...]
        inv2 = 1.0 / cnt2.astype(f32)

        @pl.when(i < 3)
        def _():
            pairs(b2_ref, wpT[...], cnt2, cosT, PT, QT, CB)

        @pl.when(i >= 3)
        def _():
            @pl.when(i == 3)
            def _():
                pair_weights(wp_ref.at[1], wcos_ref, 1, wpT, wb)

            pairs(keep.at[i - 3], wpT[...], cnt2, cosT, PT, QT, CB)

    @pl.when(i < 4)
    def _():
        state = st_ref[...]
        ctr = state.astype(bf)
        msg[...] = jnp.zeros_like(msg)
        base = lax.broadcasted_iota(jnp.int32, (1, G), 1) + 2048
        iota = lax.broadcasted_iota(jnp.int32, (256, G), 0).astype(f32).astype(bf)
        one, zero = jnp.ones((256, G), bf), jnp.zeros((256, G), bf)

        def fetch(j):
            idx = off_ref[pl.ds(j, 1), :] + base
            hi = idx >> 8
            lo = (idx & 255).astype(f32).astype(bf)
            hot = jnp.where(jnp.broadcast_to(lo, (256, G)) == iota, one, zero)
            res = jnp.dot(tall[pl.ds(pl.multiple_of(i * C, C), WIN * C), :], hot, preferred_element_type=f32)
            hib = jnp.broadcast_to(hi, (C, G))
            nb = res[:C]
            for h in range(1, WIN):
                nb = jnp.where(hib == h, res[h * C : (h + 1) * C], nb)
            return nb.astype(bf)

        def finish(j, nb, hold_gate=False):
            rows = pl.ds(pl.multiple_of(j * C, C), C)
            own = bT_ref[rows, :]
            mixed = jnp.dot(wcT_ref[...], jnp.concatenate([ctr, nb, own], axis=0), preferred_element_type=f32)
            live = jnp.broadcast_to(jnp.where(cnt > j, 0.5, 0.0), (C, G))
            gh, ch, bh = mixed[:C], mixed[C : 2 * C], mixed[2 * C :]
            gl = jnp.tanh(gh) * live + live
            msg[...] += gl * (ch * jnp.tanh(ch) + ch)
            gate = jnp.tanh(bh) * live + live
            if hold_gate:
                gts[i - 2, rows, :] = gate.astype(bf)
            else:
                ang = old_ref[rows, :] if last else olds[i, rows, :]
                up = jnp.dot(wbT_ref[...], ang, preferred_element_type=f32)
                bo_ref[rows, :] = (own.astype(f32) + up * gate).astype(bf)

        def slot(hold_gate, j, nb):
            nxt = fetch(jnp.minimum(j + 1, S - 1))
            finish(j, nb, hold_gate)
            if not last:
                angle_slot(j, PT, QT, CB, wb[...], inv2, olds.at[i + 1])
            return nxt

        if last:

            @pl.when(i < 2)
            def _():
                lax.fori_loop(0, S, functools.partial(slot, False), fetch(0), unroll=8)

            @pl.when(i >= 2)
            def _():
                lax.fori_loop(0, S, functools.partial(slot, True), fetch(0), unroll=8)

        else:
            lax.fori_loop(0, S, functools.partial(slot, False), fetch(0), unroll=8)

        summed = (msg[...] * inv).astype(bf)
        st = state + jnp.dot(waT_ref[...], summed, preferred_element_type=f32)
        so_ref[...] = st
        if last:
            e = jnp.sum((st * we[...]).reshape(8, 8, G), axis=0)
            mine[...] += e[:, :128] + e[:, 128:]
        else:
            tabs[2, pl.ds(pl.multiple_of(i * C, C), C), :] = st.astype(bf)

    if not last:

        @pl.when(i < 2)
        def _():
            keep[i] = bo_ref[...]

    if last:

        @pl.when(i == 4)
        def _():
            pl.semaphore_wait(barrier, len(greet))
            for c in hop1:
                c.start()
            near[seat] = mine[...]

        @pl.when(i == 5)
        def _():
            for c in hop1:
                c.wait()
            acc = near[0]
            for n in range(1, near.shape[0]):
                acc = acc + near[n]
            part[...] = acc
            far[chip] = acc
            for c in hop2:
                c.start()

    @pl.when(i >= 4)
    def _():
        if last:
            pairs(bT_ref, wpT[...], cnt, cosT, PT, QT, CB)
            sums(PT, QT, CB, wb, inv, angs)
            for j in range(S):
                rows = slice(j * C, (j + 1) * C)
                up = jnp.dot(wbT_ref[...], angs[rows, :], preferred_element_type=f32)
                bo_ref[rows, :] = (bT_ref[rows, :].astype(f32) + up * gts[i - 4, rows, :].astype(f32)).astype(bf)
        else:
            sums(PT, QT, CB, wb, inv2, ang_ref)

    if not last:

        @pl.when(i == 3)
        def _():
            ang_ref[...] = olds[4]

    @pl.when(i == (5 if last else 4))
    def _():
        if last:
            for c in hop2:
                c.wait()
            acc = far[0]
            for n in range(1, far.shape[0]):
                acc = acc + far[n]
            scale = 1.0 / math.sqrt(lax.axis_size("space") * lax.axis_size("rep") * 4 * G)
            en_ref[0, 0] = jnp.sum(acc) * scale
        else:
            for g in range(4):
                for c in moves(g):
                    c.wait()
            for n in range(5):
                tab_ref[n * 4 * C : (n + 1) * 4 * C, :] = tabs[n]


def gate(last, table, offT, cnt, bT, cosT, st, w_core, w_atom, w_pair, w_cos, w_bond, extra, G=256):
    layer = 1 if last else 0
    hold = lambda i: i - (i // 4) * (i - 3)
    now = (lambda i: i - 2 * (i // 4)) if last else hold
    late = (lambda i: 2 + i // 5) if last else (lambda i: (i + 1) % 4)
    two = lambda i: jnp.minimum(i, 1)
    of = lambda l, r, c: pl.BlockSpec((None, r, c), lambda i: (l, 0, 0))
    sd = jax.ShapeDtypeStruct
    dma = pltpu.SemaphoreType.DMA
    ins = [full(20 * C, G), row(S, hold), row(1, now), seg(1024, now), seg(256, late), seg(C, hold)]
    ins += [of(layer, 3 * C, 3 * C), of(layer, C, C), full(2, C, 2 * C), full(2, C), of(layer, C, C)]
    scratch = [pltpu.VMEM((C, G), f32), pltpu.VMEM((3 * C, 3 * C), bf), pltpu.VMEM((C, C), bf)] + pair_scratch(G)
    scratch += [pltpu.VMEM((C, C), bf)]
    if last:
        ins += [full(1, C), seg(1024, two)]
        outs = [seg(C, hold), seg(1024, lambda i: two(i) + (i // 4) * (i - 3)), pl.BlockSpec(memory_space=pltpu.SMEM)]
        shapes = [sd((4, C, G), f32), sd((4, 1024, G), bf), sd((1, 1), f32)]
        tile = pltpu.VMEM((8, 128), f32)
        chips = lax.axis_size("space") // 2
        seats = 2 * lax.axis_size("rep")
        scratch += [pltpu.VMEM((C, G), f32), pltpu.VMEM((2, 1024, G), bf), pltpu.VMEM((1024, G), bf)]
        scratch += [tile, pltpu.VMEM((seats, 8, 128), f32), tile, pltpu.VMEM((chips, 8, 128), f32)]
        scratch += [dma((seats - 1,)), dma((seats - 1,)), dma((chips - 1,)), dma((chips - 1,))]
    else:
        turn = lambda i: (i + 1) % 4
        ins += [full(1024, G), seg(1024, lambda i: jnp.minimum(i + 1, 3)), row(1, turn)]
        outs = [seg(C, hold), seg(1024, hold), seg(1024, lambda i: i // 4), full(20 * C, G)]
        shapes = [sd((4, C, G), f32), sd((4, 1024, G), bf), sd((2, 1024, G), bf), sd((20 * C, G), bf)]
        scratch += [pltpu.VMEM((5, 1024, G), bf), pltpu.VMEM((2, 1024, G), bf), pltpu.VMEM((5, 4 * C, G), bf)]
        scratch += [dma((4, 4)), dma((4, 4))]
    return pl.pallas_call(
        functools.partial(gate_kernel, last),
        grid=(6 if last else 5,),
        in_specs=ins,
        out_specs=outs,
        out_shape=shapes,
        scratch_shapes=scratch,
        compiler_params=pltpu.CompilerParams(collective_id=1 + layer, has_side_effects=True),
        name=f"gate_{layer}",
    )(table, offT, cnt, bT, cosT, st, w_core, w_atom, w_pair, w_cos, w_bond, *extra)


def turn_kernel(bT_ref, st_ref, so_ref, bo_ref):
    G = bT_ref.shape[1]
    so_ref[...] = st_ref[...]
    for h in range(G // 128):
        for a in range(8):
            cut = bT_ref[a * 128 : (a + 1) * 128, h * 128 : (h + 1) * 128]
            bo_ref[h * 128 : (h + 1) * 128, a * 128 : (a + 1) * 128] = cut.T


def turned(bT, st, G=256):
    step = lambda i: i
    sd = jax.ShapeDtypeStruct
    return pl.pallas_call(
        turn_kernel,
        grid=(4,),
        in_specs=[seg(1024, step), seg(C, step)],
        out_specs=[row(C, step), pl.BlockSpec((G, 1024), lambda i: (i, 0))],
        out_shape=[sd((C, 4 * G), f32), sd((4 * G, 1024), bf)],
        name="turned",
    )(bT, st)


def per_device(atoms, bonds, offsets, counts, cosines, w_core, w_atom, w_pair, w_cos, w_bond, w_energy):
    cnt = counts.reshape(1, -1)
    offT = offsets.T
    shared = (w_core, w_atom, w_pair, w_cos, w_bond)
    bT, cosT, old, table, st = first(bonds, cosines, atoms.T, cnt, w_pair, w_cos)
    st, bT, early, table = gate(False, table, offT, cnt, bT, cosT, st, *shared, (old, bT, cnt))
    st, bT, energy = gate(True, table, offT, cnt, bT, cosT, st, *shared, (w_energy.reshape(1, -1), early))
    st, bo = turned(bT, st)
    return st.T, bo, energy.reshape(())


def solution(mesh):
    both = ("space", "rep")
    return jax.shard_map(
        per_device,
        mesh=mesh,
        in_specs=(P("space", None), P(both, None), P(both, None), P(both), P(both, None)) + (P(),) * 6,
        out_specs=(P(both, None), P(both, None), P()),
        check_vma=False,
    )
```

```python
import functools
import math

import jax
import jax.numpy as jnp
from jax import lax
from jax.experimental import pallas as pl
from jax.experimental.pallas import tpu as pltpu
from jax.sharding import PartitionSpec as P

C = 64
S = 16
BIG = 1e30
WIN = 17
f32 = jnp.float32
bf = jnp.bfloat16
MESH = pl.DeviceIdType.MESH


def swap(ref, pad):
    rows, cols = ref.shape
    full = jnp.pad(ref[...].astype(f32), ((0, pad - rows), (0, pad - cols))) if (rows, cols) != (pad, pad) else ref[...]
    out = jnp.concatenate(
        [
            jnp.concatenate(
                [full[b * 128 : (b + 1) * 128, a * 128 : (a + 1) * 128].T for b in range(pad // 128)], axis=1
            )
            for a in range(pad // 128)
        ],
        axis=0,
    )
    return out[:cols, :rows]


def column(row, width):
    return jnp.broadcast_to(row, (width, C)).T


def pairs(bT, wp, cnt, cosT, PT, QT, CB):
    G = cnt.shape[1]
    for j in range(S):
        pq = jnp.dot(wp, bT[j * C : (j + 1) * C, :], preferred_element_type=f32)
        PT[j] = pq[:C].astype(bf).reshape(8, 8, G)
        QT[j] = jnp.where(cnt > j, pq[C:], -BIG).astype(bf).reshape(8, 8, G)
    for r in range(S * S):
        if r % (S + 1):
            CB[r] = jnp.broadcast_to(cosT[r : r + 1, :], (8, G)).astype(bf)


def angle_slot(j, PT, QT, CB, w, inv, ang_ref):
    G = inv.shape[1]
    p = PT[j]
    total, part, n = None, None, 0
    for d in range(1, S):
        k = (j + d) % S
        h = p + QT[k] + CB[j * S + k][None] * w
        v = h + h * jnp.tanh(h)
        part = v if part is None else part + v
        n += 1
        if n % 4 == 0 or n == S - 1:
            total = part if total is None else total + part
            part = None
    rows = pl.ds(pl.multiple_of(j * C, C), C)
    ang_ref[rows, :] = (total.reshape(C, G).astype(f32) * inv).astype(bf)


def sums(PT, QT, CB, wb, inv, ang_ref):
    def slot(j, carry):
        angle_slot(j, PT, QT, CB, wb[...], inv, ang_ref)
        return carry

    lax.fori_loop(0, S, slot, 0, unroll=2)


def pair_scratch(G):
    return [
        pltpu.VMEM((S, 8, 8, G), bf),
        pltpu.VMEM((S, 8, 8, G), bf),
        pltpu.VMEM((8, 8, G), bf),
        pltpu.VMEM((S * S, 8, G), bf),
        pltpu.VMEM((2 * C, C), bf),
    ]


def pair_weights(wp_ref, wc_ref, layer, wpT, wb):
    G = wb.shape[2]
    wpT[...] = (swap(wp_ref, 128)[:, :C] * 0.5).astype(bf)
    wb[...] = (column(wc_ref[layer : layer + 1, :], G) * 0.5).astype(bf).reshape(8, 8, G)


AROUND = (1, -1, 2, -2)


def beside(d):
    spaces, reps = lax.axis_size("space"), lax.axis_size("rep")
    to = (lax.axis_index("space") * reps + lax.axis_index("rep") + d + spaces * reps) % (spaces * reps)
    return (to // reps, to % reps)


def send(src, dst, ssem, rsem, to):
    return pltpu.make_async_remote_copy(
        src_ref=src, dst_ref=dst, send_sem=ssem, recv_sem=rsem, device_id=to, device_id_type=MESH
    )


def peers():
    space, rep = lax.axis_index("space"), lax.axis_index("rep")
    chip, core = space // 2, space % 2
    chips, reps = lax.axis_size("space") // 2, lax.axis_size("rep")
    close = []
    for dc in range(2):
        for dr in range(reps):
            if dc or dr:
                close.append((chip * 2 + (core + dc) % 2, (rep + dr) % reps))
    away = [(((chip + d) % chips) * 2 + core, rep) for d in range(1, chips)]
    return close, away, core * reps + rep, chip


def full(*s):
    return pl.BlockSpec(s, lambda i: (0,) * len(s))


def kernel(b_ref, cos_ref, at_ref, off_ref, cnt_ref, wcore_ref, watom_ref, wp_ref, wcos_ref, wbond_ref, we_ref, *rest):
    so_ref, bo_ref, en_ref = rest[:3]
    PT, QT, wb, CB, wpT = rest[3:8]
    wcT, waT, wbT, we, msg, nbs, bonds, cosT, sums_of, state_of, tab0, tab1, own, out = rest[8:22]
    mine, near, part, far = rest[22:26]
    osem, a_s, a_r, b_s, b_r, c_s, c_r, d_s, d_r = rest[26:]
    i = pl.program_id(0)
    G = msg.shape[1]
    spaces = lax.axis_size("space")
    space, rep = lax.axis_index("space"), lax.axis_index("rep")

    down = rep // 2
    ahead = ((space + 1 - 2 * down + spaces) % spaces, rep)
    behind = ((space - 1 + 2 * down + spaces) % spaces, rep)
    slab = lambda m: pl.ds(pl.multiple_of(m * 4 * C, 4 * C), 4 * C)
    edge1 = send(out.at[0], tab0.at[slab(down * (4 - rep // 3))], a_s.at[0], a_r.at[0], ahead)
    edge2 = send(out.at[1], tab0.at[slab(1 + 3 * down)], a_s.at[1], a_r.at[1], ahead)
    ends = rep % 3 == 0
    fill = pltpu.make_async_copy(at_ref, own, osem)

    def moves(g):
        def rows(m):
            return pl.ds(pl.multiple_of((m * 4 + g) * C, C), C)

        return [
            send(tab1.at[rows(2)], tab1.at[rows(2 - d)], b_s.at[n, g], b_r.at[n, g], beside(d))
            for n, d in enumerate(AROUND)
        ]

    close, away, seat, chip = peers()
    hop1 = [send(mine, near.at[seat], c_s.at[n], c_r.at[n], to) for n, to in enumerate(close)]
    hop2 = [send(part, far.at[chip], d_s.at[n], d_r.at[n], to) for n, to in enumerate(away)]

    greet = [behind] + [beside(d) for d in AROUND] + close + away
    barrier = pltpu.get_barrier_semaphore()

    def count(g):
        return cnt_ref[:, pl.ds(pl.multiple_of(g * G, G), G)]

    def pick(g):
        pairs(bonds.at[g], wpT[...], count(g), cosT.at[g], PT, QT, CB)

    def gate_weights(layer):
        wcT[...] = (swap(wcore_ref.at[layer], 256) * 0.5).astype(bf)
        waT[...] = swap(watom_ref.at[layer], 128).astype(bf)
        wbT[...] = swap(wbond_ref.at[layer], 128).astype(bf)

    def block(which, dst):
        for n in range(4):
            piece = own[:, pl.ds(pl.multiple_of((which * 4 + n) * G, G), G)]
            dst[n * C : (n + 1) * C, :] = piece.astype(bf)

    @pl.when(i == 0)
    def _():
        fill.start()
        for to in greet:
            pl.semaphore_signal(barrier, inc=1, device_id=to, device_id_type=MESH)
        pair_weights(wp_ref.at[0], wcos_ref, 0, wpT, wb)
        gate_weights(0)
        we[...] = column(we_ref[...], G)
        mine[...] = jnp.zeros_like(mine)

    @pl.when(i == 1)
    def _():
        fill.wait()
        block((1 - down) * (2 + rep), out.at[0])
        block(3 - 2 * down, out.at[1])
        for m in range(5):
            here = rep - 2 + m

            @pl.when((here >= 0) & (here <= 3))
            def _():
                block(here, tab0.at[slab(m)])

        for n in range(4):
            state_of[n] = own[:, pl.ds(pl.multiple_of((rep * 4 + n) * G, G), G)]

    @pl.when(i == 2)
    def _():
        pl.semaphore_wait(barrier, len(greet))
        edge1.start()

        @pl.when(ends)
        def _():
            edge2.start()

    @pl.when(i < 4)
    def _():
        g = (i + 1) % 4
        for a in range(8):
            bonds[g, a * 128 : (a + 1) * 128, :] = b_ref[:, a * 128 : (a + 1) * 128].T
        for a in range(2):
            cosT[g, a * 128 : (a + 1) * 128, :] = cos_ref[:, a * 128 : (a + 1) * 128].T

    @pl.when(i == 3)
    def _():
        pick(0)
        sums(PT, QT, CB, wb, 1.0 / count(0).astype(f32), sums_of.at[0])
        edge1.wait()

        @pl.when(ends)
        def _():
            edge2.wait()

    @pl.when((i >= 5) & (i <= 8))
    def _():
        for c in moves(i - 5):
            c.start()

    @pl.when((i >= 4) & (i < 7))
    def _():
        pick(i - 3)

    @pl.when(i == 7)
    def _():
        pair_weights(wp_ref.at[1], wcos_ref, 1, wpT, wb)
        pick(0)

    @pl.when(i == 9)
    def _():
        gate_weights(1)

    def gates(g, table, ang, hold_gate, beside_it):
        state = state_of[g]
        ctr = state.astype(bf)
        cnt = count(g)
        inv = 1.0 / cnt.astype(f32)
        msg[...] = jnp.zeros_like(msg)
        base = lax.broadcasted_iota(jnp.int32, (1, G), 1) + 2048
        iota = lax.broadcasted_iota(jnp.int32, (256, G), 0).astype(f32).astype(bf)
        one, zero = jnp.ones((256, G), bf), jnp.zeros((256, G), bf)

        def fetch(t):
            which = t // S
            idx = off_ref[pl.ds(t % S, 1), pl.ds(pl.multiple_of(which * G, G), G)] + base
            hi = idx >> 8
            lo = (idx & 255).astype(f32).astype(bf)
            hot = jnp.where(jnp.broadcast_to(lo, (256, G)) == iota, one, zero)
            rows = pl.ds(pl.multiple_of(which * C, C), WIN * C)
            res = jnp.dot(table[rows, :], hot, preferred_element_type=f32)
            hib = jnp.broadcast_to(hi, (C, G))
            nb = res[:C]
            for h in range(1, WIN):
                nb = jnp.where(hib == h, res[h * C : (h + 1) * C], nb)
            return nb.astype(bf)

        def slot(j, nb):
            nxt = fetch(jnp.minimum(g * S + j + 1, 4 * S - 1))
            rows = pl.ds(pl.multiple_of(j * C, C), C)
            mix = bonds[g, rows, :]
            mixed = jnp.dot(wcT[...], jnp.concatenate([ctr, nb, mix], axis=0), preferred_element_type=f32)
            live = jnp.broadcast_to(jnp.where(cnt > j, 0.5, 0.0), (C, G))
            gh, ch, bh = mixed[:C], mixed[C : 2 * C], mixed[2 * C :]
            gl = jnp.tanh(gh) * live + live
            msg[...] += gl * (ch * jnp.tanh(ch) + ch)
            gate = jnp.tanh(bh) * live + live
            if hold_gate:
                sums_of[g - 1, rows, :] = gate.astype(bf)
            else:
                up = jnp.dot(wbT[...], sums_of[ang, rows, :], preferred_element_type=f32)
                bonds[g, rows, :] = (mix.astype(f32) + up * gate).astype(bf)
            beside_it(j)
            return nxt

        @pl.when(g == 0)
        def _():
            nbs[...] = fetch(0)

        nbs[...] = lax.fori_loop(0, S, slot, nbs[...], unroll=8)
        summed = (msg[...] * inv).astype(bf)
        return state + jnp.dot(waT[...], summed, preferred_element_type=f32)

    @pl.when((i >= 4) & (i < 8))
    def _():
        g = i - 4
        inv = 1.0 / count((g + 1) % 4).astype(f32)

        def angle(j):
            angle_slot(j, PT, QT, CB, wb[...], inv, sums_of.at[g + 1])

        st = gates(g, tab0, g, False, angle)
        state_of[g] = st
        tab1[pl.ds(pl.multiple_of((8 + g) * C, C), C), :] = st.astype(bf)

    @pl.when(i == 8)
    def _():
        pick(1)
        sums(PT, QT, CB, wb, 1.0 / count(1).astype(f32), sums_of.at[0])
        for g in range(4):
            for c in moves(g):
                c.wait()

    def finish(g, st):
        so_ref[...] = st
        e = jnp.sum((st * we[...]).reshape(8, 8, G), axis=0)
        mine[...] += e[:, :128] + e[:, 128:]

    def turn(g):
        for h in range(G // 128):
            for a in range(8):
                cut = bonds[g, a * 128 : (a + 1) * 128, h * 128 : (h + 1) * 128]
                bo_ref[h * 128 : (h + 1) * 128, a * 128 : (a + 1) * 128] = cut.T

    @pl.when((i >= 9) & (i < 11))
    def _():
        g = i - 9
        finish(g, gates(g, tab1, 4 - 4 * g, False, lambda j: None))

    @pl.when((i >= 11) & (i < 13))
    def _():
        g = i - 9
        finish(g, gates(g, tab1, 0, True, lambda j: None))

    @pl.when(i == 13)
    def _():
        for c in hop1:
            c.start()
        near[seat] = mine[...]

    @pl.when(i == 14)
    def _():
        for c in hop1:
            c.wait()
        acc = near[0]
        for n in range(1, near.shape[0]):
            acc = acc + near[n]
        part[...] = acc
        far[chip] = acc
        for c in hop2:
            c.start()

    @pl.when(i >= 13)
    def _():
        g = i - 11
        pick(g)
        sums(PT, QT, CB, wb, 1.0 / count(g).astype(f32), sums_of.at[3])
        for j in range(S):
            rows = slice(j * C, (j + 1) * C)
            up = jnp.dot(wbT[...], sums_of[3, rows, :], preferred_element_type=f32)
            new = bonds[g, rows, :].astype(f32) + up * sums_of[g - 1, rows, :].astype(f32)
            bonds[g, rows, :] = new.astype(bf)

    @pl.when(((i >= 9) & (i < 11)) | (i >= 13))
    def _():
        turn(i - 9 - (i // 13) * 2)

    @pl.when(i == 14)
    def _():
        for c in hop2:
            c.wait()
        acc = far[0]
        for n in range(1, far.shape[0]):
            acc = acc + far[n]
        scale = 1.0 / math.sqrt(spaces * lax.axis_size("rep") * 4 * G)
        en_ref[0, 0] = jnp.sum(acc) * scale


def run(bonds, cos, at, offT, cnt, w_core, w_atom, w_pair, w_cos, w_bond, we, G=256):
    turn = lambda i: ((jnp.minimum(i, 3) + 1) % 4, 0)
    two = lambda i: jnp.minimum(jnp.maximum(i - 9, 0), 1)
    sd = jax.ShapeDtypeStruct
    dma = pltpu.SemaphoreType.DMA
    tile = pltpu.VMEM((8, 128), f32)
    chips = lax.axis_size("space") // 2
    seats = 2 * lax.axis_size("rep")
    return pl.pallas_call(
        kernel,
        grid=(15,),
        in_specs=[
            pl.BlockSpec((G, 1024), turn),
            pl.BlockSpec((G, 256), turn),
            pl.BlockSpec(memory_space=pl.ANY),
            full(S, 4 * G),
            full(1, 4 * G),
            full(2, 3 * C, 3 * C),
            full(2, C, C),
            full(2, C, 2 * C),
            full(2, C),
            full(2, C, C),
            full(1, C),
        ],
        out_specs=[
            pl.BlockSpec((C, G), lambda i: (0, jnp.minimum(jnp.maximum(i - 9, 0), 3))),
            pl.BlockSpec((G, 1024), lambda i: (two(i) + (i // 13) * (i - 12), 0)),
            pl.BlockSpec(memory_space=pltpu.SMEM),
        ],
        out_shape=[sd((C, 4 * G), f32), sd((4 * G, 1024), bf), sd((1, 1), f32)],
        scratch_shapes=pair_scratch(G)
        + [pltpu.VMEM((3 * C, 3 * C), bf), pltpu.VMEM((C, C), bf), pltpu.VMEM((C, C), bf), pltpu.VMEM((C, G), f32)]
        + [pltpu.VMEM((C, G), f32), pltpu.VMEM((C, G), bf), pltpu.VMEM((4, 1024, G), bf), pltpu.VMEM((4, 256, G), f32)]
        + [pltpu.VMEM((5, 1024, G), bf), pltpu.VMEM((4, C, G), f32), pltpu.VMEM((20 * C, G), bf)]
        + [pltpu.VMEM((20 * C, G), bf), pltpu.VMEM(at.shape, f32), pltpu.VMEM((2, 4 * C, G), bf)]
        + [tile, pltpu.VMEM((seats, 8, 128), f32), tile, pltpu.VMEM((chips, 8, 128), f32)]
        + [dma, dma((2,)), dma((2,)), dma((4, 4)), dma((4, 4))]
        + [dma((seats - 1,)), dma((seats - 1,)), dma((chips - 1,)), dma((chips - 1,))],
        compiler_params=pltpu.CompilerParams(collective_id=0, has_side_effects=True),
        name="layers",
    )(bonds, cos, at, offT, cnt, w_core, w_atom, w_pair, w_cos, w_bond, we)


def per_device(atoms, bonds, offsets, counts, cosines, w_core, w_atom, w_pair, w_cos, w_bond, w_energy):
    st, bo, energy = run(
        bonds,
        cosines,
        atoms.T,
        offsets.T,
        counts.reshape(1, -1),
        w_core,
        w_atom,
        w_pair,
        w_cos,
        w_bond,
        w_energy.reshape(1, -1),
    )
    return st.T, bo, energy.reshape(())


def solution(mesh):
    both = ("space", "rep")
    return jax.shard_map(
        per_device,
        mesh=mesh,
        in_specs=(P("space", None), P(both, None), P(both, None), P(both), P(both, None)) + (P(),) * 6,
        out_specs=(P(both, None), P(both, None), P()),
        check_vma=False,
    )
```

```python
import functools
import math

import jax
import jax.numpy as jnp
from jax import lax
from jax.experimental import pallas as pl
from jax.experimental.pallas import tpu as pltpu
from jax.sharding import PartitionSpec as P

C = 64
S = 16
BIG = 1e30
WIN = 17
f32 = jnp.float32
bf = jnp.bfloat16
MESH = pl.DeviceIdType.MESH
UNROLL = (4, 16)


def swap(ref, pad):
    rows, cols = ref.shape
    full = jnp.pad(ref[...].astype(f32), ((0, pad - rows), (0, pad - cols))) if (rows, cols) != (pad, pad) else ref[...]
    out = jnp.concatenate(
        [
            jnp.concatenate(
                [full[b * 128 : (b + 1) * 128, a * 128 : (a + 1) * 128].T for b in range(pad // 128)], axis=1
            )
            for a in range(pad // 128)
        ],
        axis=0,
    )
    return out[:cols, :rows]


def column(row, width):
    return jnp.broadcast_to(row, (width, C)).T


def pairs(bT, wp, cnt, cosT, PT, QT, CB):
    G = cnt.shape[1]
    for j in range(S):
        pq = jnp.dot(wp, bT[j * C : (j + 1) * C, :], preferred_element_type=f32)
        PT[j] = pq[:C].astype(bf).reshape(8, 8, G)
        QT[j] = jnp.where(cnt > j, pq[C:], -BIG).astype(bf).reshape(8, 8, G)
    for r in range(S * S):
        if r % (S + 1):
            CB[r] = jnp.broadcast_to(cosT[r : r + 1, :], (8, G)).astype(bf)


def angle_slot(j, PT, QT, CB, wb, inv, ang_ref, cuts=1):
    G = inv.shape[1]
    size = 8 // cuts
    for cut in range(cuts):
        span = slice(cut * size, (cut + 1) * size)
        p, w = PT[j, span], wb[span]
        total, part, n = None, None, 0
        for d in range(1, S):
            k = (j + d) % S
            h = p + QT[k, span] + CB[j * S + k][None] * w
            v = h + h * jnp.tanh(h)
            part = v if part is None else part + v
            n += 1
            if n % 4 == 0 or n == S - 1:
                total = part if total is None else total + part
                part = None
        rows = pl.ds(pl.multiple_of(j * C + cut * size * 8, size * 8), size * 8)
        ang_ref[rows, :] = (total.reshape(size * 8, G).astype(f32) * inv).astype(bf)


def sums(PT, QT, CB, wb, inv, ang_ref):
    def slot(j, carry):
        angle_slot(j, PT, QT, CB, wb, inv, ang_ref)
        return carry

    lax.fori_loop(0, S, slot, 0, unroll=2)


def pair_scratch(G):
    return [
        pltpu.VMEM((S, 8, 8, G), bf),
        pltpu.VMEM((S, 8, 8, G), bf),
        pltpu.VMEM((8, 8, G), bf),
        pltpu.VMEM((S * S, 8, G), bf),
        pltpu.VMEM((2 * C, C), bf),
    ]


def pair_weights(wp_ref, wc_ref, layer, wpT, wb):
    G = wb.shape[2]
    wpT[...] = (swap(wp_ref, 128)[:, :C] * 0.5).astype(bf)
    wb[...] = (column(wc_ref[layer : layer + 1, :], G) * 0.5).astype(bf).reshape(8, 8, G)


AROUND = (1, -1, 2, -2)


def beside(d):
    spaces, reps = lax.axis_size("space"), lax.axis_size("rep")
    to = (lax.axis_index("space") * reps + lax.axis_index("rep") + d + spaces * reps) % (spaces * reps)
    return (to // reps, to % reps)


def send(src, dst, ssem, rsem, to):
    return pltpu.make_async_remote_copy(
        src_ref=src, dst_ref=dst, send_sem=ssem, recv_sem=rsem, device_id=to, device_id_type=MESH
    )


def peers():
    space, rep = lax.axis_index("space"), lax.axis_index("rep")
    chip, core = space // 2, space % 2
    chips, reps = lax.axis_size("space") // 2, lax.axis_size("rep")
    close = []
    for dc in range(2):
        for dr in range(reps):
            if dc or dr:
                close.append((chip * 2 + (core + dc) % 2, (rep + dr) % reps))
    away = [(((chip + d) % chips) * 2 + core, rep) for d in range(1, chips)]
    return close, away, core * reps + rep, chip


def full(*s):
    return pl.BlockSpec(s, lambda i: (0,) * len(s))


def kernel(b_hbm, cos_hbm, at_ref, *rest):
    small, rest = rest[:8], rest[8:]
    so_ref, bo_ref, en_ref = rest[:3]
    kept, b_in, cos_in, k_sem, b_sem = rest[-12:-4], rest[-4], rest[-3], rest[-2], rest[-1]
    off_ref, cnt_ref, wcore_ref, watom_ref, wp_ref, wcos_ref, wbond_ref, we_ref = kept
    rest = rest[:-12]
    PT, QT, wb, CB, wpT = rest[3:8]
    wcT, waT, wbT, we, msg, nbs, bonds, cosT, sums_of, state_of, tab0, tab1, own, out = rest[8:22]
    mine, near, part, far = rest[22:26]
    osem, a_s, a_r, b_s, b_r, c_s, c_r, d_s, d_r = rest[26:]
    i = pl.program_id(0)
    G = msg.shape[1]
    spaces = lax.axis_size("space")
    space, rep = lax.axis_index("space"), lax.axis_index("rep")

    down = rep // 2
    ahead = ((space + 1 - 2 * down + spaces) % spaces, rep)
    behind = ((space - 1 + 2 * down + spaces) % spaces, rep)
    slab = lambda m: pl.ds(pl.multiple_of(m * 4 * C, 4 * C), 4 * C)
    edge1 = send(out.at[0], tab0.at[slab(down * (4 - rep // 3))], a_s.at[0], a_r.at[0], ahead)
    edge2 = send(out.at[1], tab0.at[slab(1 + 3 * down)], a_s.at[1], a_r.at[1], ahead)
    ends = rep % 3 == 0
    fill = pltpu.make_async_copy(at_ref, own, osem)
    loads = [pltpu.make_async_copy(a, b, k_sem.at[n]) for n, (a, b) in enumerate(zip(small, kept))]

    def rows_in(g):
        rows = pl.ds(pl.multiple_of(g * G, G), G)
        return [
            pltpu.make_async_copy(b_hbm.at[rows], b_in.at[g], b_sem.at[0, g]),
            pltpu.make_async_copy(cos_hbm.at[rows], cos_in.at[g], b_sem.at[1, g]),
        ]


    def moves(g):
        def rows(m):
            return pl.ds(pl.multiple_of((m * 4 + g) * C, C), C)

        return [
            send(tab1.at[rows(2)], tab1.at[rows(2 - d)], b_s.at[n, g], b_r.at[n, g], beside(d))
            for n, d in enumerate(AROUND)
        ]

    close, away, seat, chip = peers()
    hop1 = [send(mine, near.at[seat], c_s.at[n], c_r.at[n], to) for n, to in enumerate(close)]
    hop2 = [send(part, far.at[chip], d_s.at[n], d_r.at[n], to) for n, to in enumerate(away)]

    greet = [behind] + [beside(d) for d in AROUND] + close + away
    barrier = pltpu.get_barrier_semaphore()

    def count(g):
        return cnt_ref[:, pl.ds(pl.multiple_of(g * G, G), G)]

    def pick(g):
        pairs(bonds.at[g], wpT[...], count(g), cosT.at[g], PT, QT, CB)

    def gate_weights(layer):
        wcT[...] = (swap(wcore_ref.at[layer], 256) * 0.5).astype(bf)
        waT[...] = swap(watom_ref.at[layer], 128).astype(bf)
        wbT[...] = swap(wbond_ref.at[layer], 128).astype(bf)

    def block(which, dst):
        for n in range(4):
            piece = own[:, pl.ds(pl.multiple_of((which * 4 + n) * G, G), G)]
            dst[n * C : (n + 1) * C, :] = piece.astype(bf)

    @pl.when(i == 0)
    def _():
        for c in loads:
            c.start()
        for g in (1, 2, 3, 0):
            for c in rows_in(g):
                c.start()
            if g == 1:
                fill.start()
        for to in greet:
            pl.semaphore_signal(barrier, inc=1, device_id=to, device_id_type=MESH)
        for c in loads:
            c.wait()
        pair_weights(wp_ref.at[0], wcos_ref, 0, wpT, wb)
        gate_weights(0)
        we[...] = column(we_ref[...], G)
        mine[...] = jnp.zeros_like(mine)

    @pl.when(i == 1)
    def _():
        fill.wait()
        block((1 - down) * (2 + rep), out.at[0])
        block(3 - 2 * down, out.at[1])
        for m in range(5):
            here = rep - 2 + m

            @pl.when((here >= 0) & (here <= 3))
            def _():
                block(here, tab0.at[slab(m)])

        for n in range(4):
            state_of[n] = own[:, pl.ds(pl.multiple_of((rep * 4 + n) * G, G), G)]

    @pl.when(i == 2)
    def _():
        pl.semaphore_wait(barrier, len(greet))
        edge1.start()

        @pl.when(ends)
        def _():
            edge2.start()

    @pl.when(i < 4)
    def _():
        g = (i + 1) % 4
        for c in rows_in(g):
            c.wait()
        for a in range(8):
            bonds[g, a * 128 : (a + 1) * 128, :] = b_in[g, :, a * 128 : (a + 1) * 128].T
        for a in range(2):
            cosT[g, a * 128 : (a + 1) * 128, :] = cos_in[g, :, a * 128 : (a + 1) * 128].T

    @pl.when(i == 3)
    def _():
        pick(0)
        sums(PT, QT, CB, wb, 1.0 / count(0).astype(f32), sums_of.at[0])
        edge1.wait()

        @pl.when(ends)
        def _():
            edge2.wait()

    @pl.when((i >= 5) & (i <= 8))
    def _():
        for c in moves(i - 5):
            c.start()

    @pl.when((i >= 4) & (i < 7))
    def _():
        pick(i - 3)

    @pl.when(i == 7)
    def _():
        pair_weights(wp_ref.at[1], wcos_ref, 1, wpT, wb)
        pick(0)

    @pl.when(i == 9)
    def _():
        gate_weights(1)

    def gates(layer, g, table, ang, hold_gate, beside_it):
        state = state_of[g]
        ctr = state.astype(bf)
        cnt = count(g)
        inv = 1.0 / cnt.astype(f32)
        msg[...] = jnp.zeros_like(msg)
        base = lax.broadcasted_iota(jnp.int32, (1, G), 1) + 2048
        iota = lax.broadcasted_iota(jnp.int32, (256, G), 0).astype(f32).astype(bf)
        one, zero = jnp.ones((256, G), bf), jnp.zeros((256, G), bf)

        def fetch(t):
            which = t // S
            idx = off_ref[pl.ds(t % S, 1), pl.ds(pl.multiple_of(which * G, G), G)] + base
            hi = idx >> 8
            lo = (idx & 255).astype(f32).astype(bf)
            hot = jnp.where(jnp.broadcast_to(lo, (256, G)) == iota, one, zero)
            rows = pl.ds(pl.multiple_of(which * C, C), WIN * C)
            res = jnp.dot(table[rows, :], hot, preferred_element_type=f32)
            hib = jnp.broadcast_to(hi, (C, G))
            nb = res[:C]
            for h in range(1, WIN):
                nb = jnp.where(hib == h, res[h * C : (h + 1) * C], nb)
            return nb.astype(bf)

        def slot(j, nb):
            nxt = fetch(jnp.minimum(g * S + j + 1, 4 * S - 1))
            rows = pl.ds(pl.multiple_of(j * C, C), C)
            mix = bonds[g, rows, :]
            mixed = jnp.dot(wcT[...], jnp.concatenate([ctr, nb, mix], axis=0), preferred_element_type=f32)
            live = jnp.broadcast_to(jnp.where(cnt > j, 0.5, 0.0), (C, G))
            gh, ch, bh = mixed[:C], mixed[C : 2 * C], mixed[2 * C :]
            gl = jnp.tanh(gh) * live + live
            msg[...] += gl * (ch * jnp.tanh(ch) + ch)
            gate = jnp.tanh(bh) * live + live
            if hold_gate:
                sums_of[g - 1, rows, :] = gate.astype(bf)
            else:
                up = jnp.dot(wbT[...], sums_of[ang, rows, :], preferred_element_type=f32)
                bonds[g, rows, :] = (mix.astype(f32) + up * gate).astype(bf)
            beside_it(j)
            return nxt

        @pl.when(g == 0)
        def _():
            nbs[...] = fetch(0)

        nbs[...] = lax.fori_loop(0, S, slot, nbs[...], unroll=UNROLL[layer])
        summed = (msg[...] * inv).astype(bf)
        return state + jnp.dot(waT[...], summed, preferred_element_type=f32)

    @pl.when((i >= 4) & (i < 8))
    def _():
        g = i - 4
        inv = 1.0 / count((g + 1) % 4).astype(f32)

        def angle(j):
            angle_slot(j, PT, QT, CB, wb, inv, sums_of.at[g + 1], 2)

        st = gates(0, g, tab0, g, False, angle)
        state_of[g] = st
        tab1[pl.ds(pl.multiple_of((8 + g) * C, C), C), :] = st.astype(bf)

    @pl.when(i == 8)
    def _():
        pick(1)
        sums(PT, QT, CB, wb, 1.0 / count(1).astype(f32), sums_of.at[0])
        for g in range(4):
            for c in moves(g):
                c.wait()

    def finish(g, st):
        so_ref[...] = st
        e = jnp.sum((st * we[...]).reshape(8, 8, G), axis=0)
        mine[...] += e[:, :128] + e[:, 128:]

    def turn(g):
        for h in range(G // 128):
            for a in range(8):
                cut = bonds[g, a * 128 : (a + 1) * 128, h * 128 : (h + 1) * 128]
                bo_ref[h * 128 : (h + 1) * 128, a * 128 : (a + 1) * 128] = cut.T

    @pl.when((i >= 9) & (i < 11))
    def _():
        g = i - 9
        finish(g, gates(1, g, tab1, 4 - 4 * g, False, lambda j: None))

    @pl.when((i >= 11) & (i < 13))
    def _():
        g = i - 9
        finish(g, gates(1, g, tab1, 0, True, lambda j: None))

    @pl.when(i == 13)
    def _():
        for c in hop1:
            c.start()
        near[seat] = mine[...]

    @pl.when(i == 14)
    def _():
        for c in hop1:
            c.wait()
        acc = near[0]
        for n in range(1, near.shape[0]):
            acc = acc + near[n]
        part[...] = acc
        far[chip] = acc
        for c in hop2:
            c.start()

    @pl.when(i >= 13)
    def _():
        g = i - 11
        pick(g)
        sums(PT, QT, CB, wb, 1.0 / count(g).astype(f32), sums_of.at[3])
        for j in range(S):
            rows = slice(j * C, (j + 1) * C)
            up = jnp.dot(wbT[...], sums_of[3, rows, :], preferred_element_type=f32)
            new = bonds[g, rows, :].astype(f32) + up * sums_of[g - 1, rows, :].astype(f32)
            bonds[g, rows, :] = new.astype(bf)

    @pl.when(((i >= 9) & (i < 11)) | (i >= 13))
    def _():
        turn(i - 9 - (i // 13) * 2)

    @pl.when(i == 14)
    def _():
        for c in hop2:
            c.wait()
        acc = far[0]
        for n in range(1, far.shape[0]):
            acc = acc + far[n]
        scale = 1.0 / math.sqrt(spaces * lax.axis_size("rep") * 4 * G)
        en_ref[0, 0] = jnp.sum(acc) * scale


def run(bonds, cos, at, *small, G=256):
    two = lambda i: jnp.minimum(jnp.maximum(i - 9, 0), 1)
    sd = jax.ShapeDtypeStruct
    dma = pltpu.SemaphoreType.DMA
    tile = pltpu.VMEM((8, 128), f32)
    chips = lax.axis_size("space") // 2
    seats = 2 * lax.axis_size("rep")
    return pl.pallas_call(
        kernel,
        grid=(15,),
        in_specs=[pl.BlockSpec(memory_space=pltpu.HBM)] * 11,
        out_specs=[
            pl.BlockSpec((C, G), lambda i: (0, jnp.minimum(jnp.maximum(i - 9, 0), 3))),
            pl.BlockSpec((G, 1024), lambda i: (two(i) + (i // 13) * (i - 12), 0)),
            pl.BlockSpec(memory_space=pltpu.SMEM),
        ],
        out_shape=[sd((C, 4 * G), f32), sd((4 * G, 1024), bf), sd((1, 1), f32)],
        scratch_shapes=pair_scratch(G)
        + [pltpu.VMEM((3 * C, 3 * C), bf), pltpu.VMEM((C, C), bf), pltpu.VMEM((C, C), bf), pltpu.VMEM((C, G), f32)]
        + [pltpu.VMEM((C, G), f32), pltpu.VMEM((C, G), bf), pltpu.VMEM((4, 1024, G), bf), pltpu.VMEM((4, 256, G), f32)]
        + [pltpu.VMEM((5, 1024, G), bf), pltpu.VMEM((4, C, G), f32), pltpu.VMEM((20 * C, G), bf)]
        + [pltpu.VMEM((20 * C, G), bf), pltpu.VMEM(at.shape, f32), pltpu.VMEM((2, 4 * C, G), bf)]
        + [tile, pltpu.VMEM((seats, 8, 128), f32), tile, pltpu.VMEM((chips, 8, 128), f32)]
        + [dma, dma((2,)), dma((2,)), dma((4, 4)), dma((4, 4))]
        + [dma((seats - 1,)), dma((seats - 1,)), dma((chips - 1,)), dma((chips - 1,))]
        + [pltpu.VMEM(x.shape, x.dtype) for x in small]
        + [pltpu.VMEM((4, G, 1024), bf), pltpu.VMEM((4, G, 256), f32), dma((8,)), dma((2, 4))],
        compiler_params=pltpu.CompilerParams(collective_id=0, has_side_effects=True),
        name="layers",
    )(bonds, cos, at, *small)


def per_device(atoms, bonds, offsets, counts, cosines, w_core, w_atom, w_pair, w_cos, w_bond, w_energy):
    st, bo, energy = run(
        bonds,
        cosines,
        atoms.T,
        offsets.T,
        counts.reshape(1, -1),
        w_core,
        w_atom,
        w_pair,
        w_cos,
        w_bond,
        w_energy.reshape(1, -1),
    )
    return st.T, bo, energy.reshape(())


def solution(mesh):
    both = ("space", "rep")
    return jax.shard_map(
        per_device,
        mesh=mesh,
        in_specs=(P("space", None), P(both, None), P(both, None), P(both), P(both, None)) + (P(),) * 6,
        out_specs=(P(both, None), P(both, None), P()),
        check_vma=False,
    )
```

```python
import functools
import math

import jax
import jax.numpy as jnp
from jax import lax
from jax.experimental import pallas as pl
from jax.experimental.pallas import tpu as pltpu
from jax.sharding import PartitionSpec as P

C = 64
S = 16
BIG = 1e30
WIN = 17
f32 = jnp.float32
bf = jnp.bfloat16
MESH = pl.DeviceIdType.MESH
UNROLL = (4, 16)


def swap(ref, pad):
    rows, cols = ref.shape
    full = jnp.pad(ref[...].astype(f32), ((0, pad - rows), (0, pad - cols))) if (rows, cols) != (pad, pad) else ref[...]
    out = jnp.concatenate(
        [
            jnp.concatenate(
                [full[b * 128 : (b + 1) * 128, a * 128 : (a + 1) * 128].T for b in range(pad // 128)], axis=1
            )
            for a in range(pad // 128)
        ],
        axis=0,
    )
    return out[:cols, :rows]


def column(row, width):
    return jnp.broadcast_to(row, (width, C)).T


def pairs(bT, wp, cnt, PT, QT):
    G = cnt.shape[1]
    for j in range(S):
        pq = jnp.dot(wp, bT[j * C : (j + 1) * C, :], preferred_element_type=f32)
        PT[j] = pq[:C].astype(bf).reshape(8, 8, G)
        QT[j] = jnp.where(cnt > j, pq[C:], -BIG).astype(bf).reshape(8, 8, G)


def angle_slot(j, PT, QT, CB, wb, inv, ang_ref, cuts=1):
    G = inv.shape[1]
    size = 8 // cuts
    for cut in range(cuts):
        span = slice(cut * size, (cut + 1) * size)
        p, w = PT[j, span], wb[span]
        total, part, n = None, None, 0
        for d in range(1, S):
            k = (j + d) % S
            h = p + QT[k, span] + CB[j * S + k][None] * w
            v = h + h * jnp.tanh(h)
            part = v if part is None else part + v
            n += 1
            if n % 4 == 0 or n == S - 1:
                total = part if total is None else total + part
                part = None
        rows = pl.ds(pl.multiple_of(j * C + cut * size * 8, size * 8), size * 8)
        ang_ref[rows, :] = (total.reshape(size * 8, G).astype(f32) * inv).astype(bf)


def sums(PT, QT, CB, wb, inv, ang_ref):
    def slot(j, carry):
        angle_slot(j, PT, QT, CB, wb, inv, ang_ref)
        return carry

    lax.fori_loop(0, S, slot, 0, unroll=2)


def pair_scratch(G):
    return [
        pltpu.VMEM((S, 8, 8, G), bf),
        pltpu.VMEM((S, 8, 8, G), bf),
        pltpu.VMEM((8, 8, G), bf),
        pltpu.VMEM((4, S * S, 8, G), bf),
        pltpu.VMEM((2 * C, C), bf),
    ]


def pair_weights(wp_ref, wc_ref, layer, wpT, wb):
    G = wb.shape[2]
    wpT[...] = (swap(wp_ref, 128)[:, :C] * 0.5).astype(bf)
    wb[...] = (column(wc_ref[layer : layer + 1, :], G) * 0.5).astype(bf).reshape(8, 8, G)


AROUND = (1, -1, 2, -2)


def beside(d):
    spaces, reps = lax.axis_size("space"), lax.axis_size("rep")
    to = (lax.axis_index("space") * reps + lax.axis_index("rep") + d + spaces * reps) % (spaces * reps)
    return (to // reps, to % reps)


def send(src, dst, ssem, rsem, to):
    return pltpu.make_async_remote_copy(
        src_ref=src, dst_ref=dst, send_sem=ssem, recv_sem=rsem, device_id=to, device_id_type=MESH
    )


def peers():
    space, rep = lax.axis_index("space"), lax.axis_index("rep")
    chip, core = space // 2, space % 2
    chips, reps = lax.axis_size("space") // 2, lax.axis_size("rep")
    close = []
    for dc in range(2):
        for dr in range(reps):
            if dc or dr:
                close.append((chip * 2 + (core + dc) % 2, (rep + dr) % reps))
    away = [(((chip + d) % chips) * 2 + core, rep) for d in range(1, chips)]
    return close, away, core * reps + rep, chip


def full(*s):
    return pl.BlockSpec(s, lambda i: (0,) * len(s))


def kernel(b_hbm, cos_hbm, at_ref, *rest):
    small, rest = rest[:8], rest[8:]
    so_ref, bo_ref, en_ref = rest[:3]
    kept, b_in, cos_in, k_sem, b_sem = rest[-12:-4], rest[-4], rest[-3], rest[-2], rest[-1]
    off_ref, cnt_ref, wcore_ref, watom_ref, wp_ref, wcos_ref, wbond_ref, we_ref = kept
    rest = rest[:-12]
    PT, QT, wb, CB, wpT = rest[3:8]
    wcT, waT, wbT, we, msg, nbs, bonds, cosT, sums_of, state_of, tab0, tab1, own, out = rest[8:22]
    mine, near, part, far = rest[22:26]
    osem, a_s, a_r, b_s, b_r, c_s, c_r, d_s, d_r = rest[26:]
    i = pl.program_id(0)
    G = msg.shape[1]
    spaces = lax.axis_size("space")
    space, rep = lax.axis_index("space"), lax.axis_index("rep")

    down = rep // 2
    ahead = ((space + 1 - 2 * down + spaces) % spaces, rep)
    behind = ((space - 1 + 2 * down + spaces) % spaces, rep)
    slab = lambda m: pl.ds(pl.multiple_of(m * 4 * C, 4 * C), 4 * C)
    edge1 = send(out.at[0], tab0.at[slab(down * (4 - rep // 3))], a_s.at[0], a_r.at[0], ahead)
    edge2 = send(out.at[1], tab0.at[slab(1 + 3 * down)], a_s.at[1], a_r.at[1], ahead)
    ends = rep % 3 == 0
    fill = pltpu.make_async_copy(at_ref, own, osem)
    loads = [pltpu.make_async_copy(a, b, k_sem.at[n]) for n, (a, b) in enumerate(zip(small, kept))]

    def rows_in(g):
        rows = pl.ds(pl.multiple_of(g * G, G), G)
        return [
            pltpu.make_async_copy(b_hbm.at[rows], b_in.at[g], b_sem.at[0, g]),
            pltpu.make_async_copy(cos_hbm.at[rows], cos_in.at[g], b_sem.at[1, g]),
        ]


    def moves(g):
        def rows(m):
            return pl.ds(pl.multiple_of((m * 4 + g) * C, C), C)

        return [
            send(tab1.at[rows(2)], tab1.at[rows(2 - d)], b_s.at[n, g], b_r.at[n, g], beside(d))
            for n, d in enumerate(AROUND)
        ]

    close, away, seat, chip = peers()
    hop1 = [send(mine, near.at[seat], c_s.at[n], c_r.at[n], to) for n, to in enumerate(close)]
    hop2 = [send(part, far.at[chip], d_s.at[n], d_r.at[n], to) for n, to in enumerate(away)]

    greet = [behind] + [beside(d) for d in AROUND] + close + away
    barrier = pltpu.get_barrier_semaphore()

    def count(g):
        return cnt_ref[:, pl.ds(pl.multiple_of(g * G, G), G)]

    def pick(g):
        pairs(bonds.at[g], wpT[...], count(g), PT, QT)

    def gate_weights(layer):
        wcT[...] = (swap(wcore_ref.at[layer], 256) * 0.5).astype(bf)
        waT[...] = swap(watom_ref.at[layer], 128).astype(bf)
        wbT[...] = swap(wbond_ref.at[layer], 128).astype(bf)

    def block(which, dst):
        for n in range(4):
            piece = own[:, pl.ds(pl.multiple_of((which * 4 + n) * G, G), G)]
            dst[n * C : (n + 1) * C, :] = piece.astype(bf)

    @pl.when(i == 0)
    def _():
        for c in loads:
            c.start()
        for g in (1, 2, 3, 0):
            for c in rows_in(g):
                c.start()
            if g == 1:
                fill.start()
        for to in greet:
            pl.semaphore_signal(barrier, inc=1, device_id=to, device_id_type=MESH)
        for c in loads:
            c.wait()
        pair_weights(wp_ref.at[0], wcos_ref, 0, wpT, wb)
        gate_weights(0)
        we[...] = column(we_ref[...], G)
        mine[...] = jnp.zeros_like(mine)

    @pl.when(i == 1)
    def _():
        fill.wait()
        block((1 - down) * (2 + rep), out.at[0])
        block(3 - 2 * down, out.at[1])
        for m in range(5):
            here = rep - 2 + m

            @pl.when((here >= 0) & (here <= 3))
            def _():
                block(here, tab0.at[slab(m)])

        for n in range(4):
            state_of[n] = own[:, pl.ds(pl.multiple_of((rep * 4 + n) * G, G), G)]

    @pl.when(i == 2)
    def _():
        pl.semaphore_wait(barrier, len(greet))
        edge1.start()

        @pl.when(ends)
        def _():
            edge2.start()

    @pl.when(i < 4)
    def _():
        g = (i + 1) % 4
        for c in rows_in(g):
            c.wait()
        for a in range(8):
            bonds[g, a * 128 : (a + 1) * 128, :] = b_in[g, :, a * 128 : (a + 1) * 128].T
        for a in range(2):
            cosT[a * 128 : (a + 1) * 128, :] = cos_in[g, :, a * 128 : (a + 1) * 128].T
        for r in range(S * S):
            if r % (S + 1):
                CB[g, r] = jnp.broadcast_to(cosT[r : r + 1, :], (8, G)).astype(bf)

    @pl.when(i == 3)
    def _():
        pick(0)
        sums(PT, QT, CB.at[0], wb, 1.0 / count(0).astype(f32), sums_of.at[0])
        edge1.wait()

        @pl.when(ends)
        def _():
            edge2.wait()

    @pl.when((i >= 5) & (i <= 8))
    def _():
        for c in moves(i - 5):
            c.start()

    @pl.when((i >= 4) & (i < 7))
    def _():
        pick(i - 3)

    @pl.when(i == 7)
    def _():
        pair_weights(wp_ref.at[1], wcos_ref, 1, wpT, wb)
        pick(0)

    @pl.when(i == 9)
    def _():
        gate_weights(1)

    def gates(layer, g, table, ang, hold_gate, beside_it):
        state = state_of[g]
        ctr = state.astype(bf)
        cnt = count(g)
        inv = 1.0 / cnt.astype(f32)
        msg[...] = jnp.zeros_like(msg)
        base = lax.broadcasted_iota(jnp.int32, (1, G), 1) + 2048
        iota = lax.broadcasted_iota(jnp.int32, (256, G), 0).astype(f32).astype(bf)
        one, zero = jnp.ones((256, G), bf), jnp.zeros((256, G), bf)

        def fetch(t):
            which = t // S
            idx = off_ref[pl.ds(t % S, 1), pl.ds(pl.multiple_of(which * G, G), G)] + base
            hi = idx >> 8
            lo = (idx & 255).astype(f32).astype(bf)
            hot = jnp.where(jnp.broadcast_to(lo, (256, G)) == iota, one, zero)
            rows = pl.ds(pl.multiple_of(which * C, C), WIN * C)
            res = jnp.dot(table[rows, :], hot, preferred_element_type=f32)
            hib = jnp.broadcast_to(hi, (C, G))
            nb = res[:C]
            for h in range(1, WIN):
                nb = jnp.where(hib == h, res[h * C : (h + 1) * C], nb)
            return nb.astype(bf)

        def slot(j, nb):
            nxt = fetch(jnp.minimum(g * S + j + 1, 4 * S - 1))
            rows = pl.ds(pl.multiple_of(j * C, C), C)
            mix = bonds[g, rows, :]
            mixed = jnp.dot(wcT[...], jnp.concatenate([ctr, nb, mix], axis=0), preferred_element_type=f32)
            live = jnp.broadcast_to(jnp.where(cnt > j, 0.5, 0.0), (C, G))
            gh, ch, bh = mixed[:C], mixed[C : 2 * C], mixed[2 * C :]
            gl = jnp.tanh(gh) * live + live
            msg[...] += gl * (ch * jnp.tanh(ch) + ch)
            gate = jnp.tanh(bh) * live + live
            if hold_gate:
                sums_of[g - 1, rows, :] = gate.astype(bf)
            else:
                up = jnp.dot(wbT[...], sums_of[ang, rows, :], preferred_element_type=f32)
                bonds[g, rows, :] = (mix.astype(f32) + up * gate).astype(bf)
            beside_it(j)
            return nxt

        @pl.when(g == 0)
        def _():
            nbs[...] = fetch(0)

        nbs[...] = lax.fori_loop(0, S, slot, nbs[...], unroll=UNROLL[layer])
        summed = (msg[...] * inv).astype(bf)
        return state + jnp.dot(waT[...], summed, preferred_element_type=f32)

    @pl.when((i >= 4) & (i < 8))
    def _():
        g = i - 4
        inv = 1.0 / count((g + 1) % 4).astype(f32)

        def angle(j):
            angle_slot(j, PT, QT, CB.at[(g + 1) % 4], wb, inv, sums_of.at[g + 1], 2)

        st = gates(0, g, tab0, g, False, angle)
        state_of[g] = st
        tab1[pl.ds(pl.multiple_of((8 + g) * C, C), C), :] = st.astype(bf)

    @pl.when(i == 8)
    def _():
        pick(1)
        sums(PT, QT, CB.at[1], wb, 1.0 / count(1).astype(f32), sums_of.at[0])
        for g in range(4):
            for c in moves(g):
                c.wait()

    def finish(g, st):
        so_ref[...] = st
        e = jnp.sum((st * we[...]).reshape(8, 8, G), axis=0)
        mine[...] += e[:, :128] + e[:, 128:]

    def turn(g):
        for h in range(G // 128):
            for a in range(8):
                cut = bonds[g, a * 128 : (a + 1) * 128, h * 128 : (h + 1) * 128]
                bo_ref[h * 128 : (h + 1) * 128, a * 128 : (a + 1) * 128] = cut.T

    @pl.when((i >= 9) & (i < 11))
    def _():
        g = i - 9
        finish(g, gates(1, g, tab1, 4 - 4 * g, False, lambda j: None))

    @pl.when((i >= 11) & (i < 13))
    def _():
        g = i - 9
        finish(g, gates(1, g, tab1, 0, True, lambda j: None))

    @pl.when(i == 13)
    def _():
        for c in hop1:
            c.start()
        near[seat] = mine[...]

    @pl.when(i >= 13)
    def _():
        g = i - 11
        pick(g)
        sums(PT, QT, CB.at[g], wb, 1.0 / count(g).astype(f32), sums_of.at[3])

    @pl.when(i == 13)
    def _():
        for c in hop1:
            c.wait()
        acc = near[0]
        for n in range(1, near.shape[0]):
            acc = acc + near[n]
        part[...] = acc
        far[chip] = acc
        for c in hop2:
            c.start()

    @pl.when(i >= 13)
    def _():
        g = i - 11
        for j in range(S):
            rows = slice(j * C, (j + 1) * C)
            up = jnp.dot(wbT[...], sums_of[3, rows, :], preferred_element_type=f32)
            new = bonds[g, rows, :].astype(f32) + up * sums_of[g - 1, rows, :].astype(f32)
            bonds[g, rows, :] = new.astype(bf)

    @pl.when(((i >= 9) & (i < 11)) | (i >= 13))
    def _():
        turn(i - 9 - (i // 13) * 2)

    @pl.when(i == 14)
    def _():
        for c in hop2:
            c.wait()
        acc = far[0]
        for n in range(1, far.shape[0]):
            acc = acc + far[n]
        scale = 1.0 / math.sqrt(spaces * lax.axis_size("rep") * 4 * G)
        en_ref[0, 0] = jnp.sum(acc) * scale


def run(bonds, cos, at, *small, G=256):
    two = lambda i: jnp.minimum(jnp.maximum(i - 9, 0), 1)
    sd = jax.ShapeDtypeStruct
    dma = pltpu.SemaphoreType.DMA
    tile = pltpu.VMEM((8, 128), f32)
    chips = lax.axis_size("space") // 2
    seats = 2 * lax.axis_size("rep")
    return pl.pallas_call(
        kernel,
        grid=(15,),
        in_specs=[pl.BlockSpec(memory_space=pltpu.HBM)] * 11,
        out_specs=[
            pl.BlockSpec((C, G), lambda i: (0, jnp.minimum(jnp.maximum(i - 9, 0), 3))),
            pl.BlockSpec((G, 1024), lambda i: (two(i) + (i // 13) * (i - 12), 0)),
            pl.BlockSpec(memory_space=pltpu.SMEM),
        ],
        out_shape=[sd((C, 4 * G), f32), sd((4 * G, 1024), bf), sd((1, 1), f32)],
        scratch_shapes=pair_scratch(G)
        + [pltpu.VMEM((3 * C, 3 * C), bf), pltpu.VMEM((C, C), bf), pltpu.VMEM((C, C), bf), pltpu.VMEM((C, G), f32)]
        + [pltpu.VMEM((C, G), f32), pltpu.VMEM((C, G), bf), pltpu.VMEM((4, 1024, G), bf), pltpu.VMEM((256, G), f32)]
        + [pltpu.VMEM((5, 1024, G), bf), pltpu.VMEM((4, C, G), f32), pltpu.VMEM((20 * C, G), bf)]
        + [pltpu.VMEM((20 * C, G), bf), pltpu.VMEM(at.shape, f32), pltpu.VMEM((2, 4 * C, G), bf)]
        + [tile, pltpu.VMEM((seats, 8, 128), f32), tile, pltpu.VMEM((chips, 8, 128), f32)]
        + [dma, dma((2,)), dma((2,)), dma((4, 4)), dma((4, 4))]
        + [dma((seats - 1,)), dma((seats - 1,)), dma((chips - 1,)), dma((chips - 1,))]
        + [pltpu.VMEM(x.shape, x.dtype) for x in small]
        + [pltpu.VMEM((4, G, 1024), bf), pltpu.VMEM((4, G, 256), f32), dma((8,)), dma((2, 4))],
        compiler_params=pltpu.CompilerParams(collective_id=0, has_side_effects=True),
        name="layers",
    )(bonds, cos, at, *small)


def flush_kernel(st_ref, bonds_ref, so_ref, bo_ref, st, rows, sem):
    n = rows.shape[0]
    size = rows.shape[1]
    ins, outs = [], []
    for k in range(n):
        part = pl.ds(k * size, size)
        ins.append(pltpu.make_async_copy(bonds_ref.at[part], rows.at[k], sem.at[0, k]))
        outs.append(pltpu.make_async_copy(rows.at[k], bo_ref.at[part], sem.at[1, k]))
    ins.append(pltpu.make_async_copy(st_ref, st, sem.at[0, n]))
    outs.append(pltpu.make_async_copy(st, so_ref, sem.at[1, n]))
    for c in ins:
        c.start()
    for c, d in zip(ins, outs):
        c.wait()
        d.start()
    for d in outs:
        d.wait()


def flush(st, bonds, n=8):
    sd = jax.ShapeDtypeStruct
    return pl.pallas_call(
        flush_kernel,
        in_specs=[pl.BlockSpec(memory_space=pl.ANY)] * 2,
        out_specs=[pl.BlockSpec(memory_space=pl.ANY)] * 2,
        out_shape=[sd(st.shape, st.dtype), sd(bonds.shape, bonds.dtype)],
        scratch_shapes=[
            pltpu.VMEM(st.shape, st.dtype),
            pltpu.VMEM((n, bonds.shape[0] // n, bonds.shape[1]), bonds.dtype),
            pltpu.SemaphoreType.DMA((2, n + 1)),
        ],
        name="flush",
    )(st, bonds)


def per_device(atoms, bonds, offsets, counts, cosines, w_core, w_atom, w_pair, w_cos, w_bond, w_energy):
    st, bo, energy = run(
        bonds,
        cosines,
        atoms.T,
        offsets.T,
        counts.reshape(1, -1),
        w_core,
        w_atom,
        w_pair,
        w_cos,
        w_bond,
        w_energy.reshape(1, -1),
    )
    st, bo = flush(st, bo)
    return st.T, bo, energy.reshape(())


def solution(mesh):
    both = ("space", "rep")
    return jax.shard_map(
        per_device,
        mesh=mesh,
        in_specs=(P("space", None), P(both, None), P(both, None), P(both), P(both, None)) + (P(),) * 6,
        out_specs=(P(both, None), P(both, None), P()),
        check_vma=False,
    )
```

```python
import functools
import math

import jax
import jax.numpy as jnp
from jax import lax
from jax.experimental import pallas as pl
from jax.experimental.pallas import tpu as pltpu
from jax.sharding import PartitionSpec as P

C = 64
S = 16
BIG = 1e30
WIN = 17
f32 = jnp.float32
bf = jnp.bfloat16
MESH = pl.DeviceIdType.MESH
UNROLL = (4, 16)


def swap(ref, pad):
    rows, cols = ref.shape
    full = jnp.pad(ref[...].astype(f32), ((0, pad - rows), (0, pad - cols))) if (rows, cols) != (pad, pad) else ref[...]
    out = jnp.concatenate(
        [
            jnp.concatenate(
                [full[b * 128 : (b + 1) * 128, a * 128 : (a + 1) * 128].T for b in range(pad // 128)], axis=1
            )
            for a in range(pad // 128)
        ],
        axis=0,
    )
    return out[:cols, :rows]


def column(row, width):
    return jnp.broadcast_to(row, (width, C)).T


def pairs(bT, wp, cnt, PT, QT):
    G = cnt.shape[1]
    for j in range(S):
        pq = jnp.dot(wp, bT[j * C : (j + 1) * C, :], preferred_element_type=f32)
        PT[j] = pq[:C].astype(bf).reshape(8, 8, G)
        QT[j] = jnp.where(cnt > j, pq[C:], -BIG).astype(bf).reshape(8, 8, G)


def angle_slot(j, PT, QT, CB, wb, inv, ang_ref, cuts=1):
    G = inv.shape[1]
    size = 8 // cuts
    for cut in range(cuts):
        span = slice(cut * size, (cut + 1) * size)
        p, w = PT[j, span], wb[span]
        total, part, n = None, None, 0
        for d in range(1, S):
            k = (j + d) % S
            h = p + QT[k, span] + CB[j * S + k][None] * w
            v = h + h * jnp.tanh(h)
            part = v if part is None else part + v
            n += 1
            if n % 4 == 0 or n == S - 1:
                total = part if total is None else total + part
                part = None
        rows = pl.ds(pl.multiple_of(j * C + cut * size * 8, size * 8), size * 8)
        ang_ref[rows, :] = (total.reshape(size * 8, G).astype(f32) * inv).astype(bf)


def sums(PT, QT, CB, wb, inv, ang_ref):
    def slot(j, carry):
        angle_slot(j, PT, QT, CB, wb, inv, ang_ref)
        return carry

    lax.fori_loop(0, S, slot, 0, unroll=2)


def pair_scratch(G):
    return [
        pltpu.VMEM((S, 8, 8, G), bf),
        pltpu.VMEM((S, 8, 8, G), bf),
        pltpu.VMEM((8, 8, G), bf),
        pltpu.VMEM((4, S * S, 8, G), bf),
        pltpu.VMEM((2 * C, C), bf),
    ]


def pair_weights(wp_ref, wc_ref, layer, wpT, wb):
    G = wb.shape[2]
    wpT[...] = (swap(wp_ref, 128)[:, :C] * 0.5).astype(bf)
    wb[...] = (column(wc_ref[layer : layer + 1, :], G) * 0.5).astype(bf).reshape(8, 8, G)


AROUND = (1, -1, 2, -2)


def beside(d):
    spaces, reps = lax.axis_size("space"), lax.axis_size("rep")
    to = (lax.axis_index("space") * reps + lax.axis_index("rep") + d + spaces * reps) % (spaces * reps)
    return (to // reps, to % reps)


def send(src, dst, ssem, rsem, to):
    return pltpu.make_async_remote_copy(
        src_ref=src, dst_ref=dst, send_sem=ssem, recv_sem=rsem, device_id=to, device_id_type=MESH
    )


def peers():
    space, rep = lax.axis_index("space"), lax.axis_index("rep")
    chip, core = space // 2, space % 2
    chips, reps = lax.axis_size("space") // 2, lax.axis_size("rep")
    close = []
    for dc in range(2):
        for dr in range(reps):
            if dc or dr:
                close.append((chip * 2 + (core + dc) % 2, (rep + dr) % reps))
    away = [(((chip + d) % chips) * 2 + core, rep) for d in range(1, chips)]
    return close, away, core * reps + rep, chip


def full(*s):
    return pl.BlockSpec(s, lambda i: (0,) * len(s))


def kernel(b_hbm, cos_hbm, at_ref, *rest):
    small, rest = rest[:8], rest[8:]
    so_ref, bo_ref, en_ref = rest[:3]
    kept, b_in, cos_in, k_sem, b_sem = rest[-12:-4], rest[-4], rest[-3], rest[-2], rest[-1]
    off_ref, cnt_ref, wcore_ref, watom_ref, wp_ref, wcos_ref, wbond_ref, we_ref = kept
    rest = rest[:-12]
    PT, QT, wb, CB, wpT = rest[3:8]
    wcT, waT, wbT, we, msg, nbs, bonds, cosT, sums_of, state_of, tab0, tab1, own, out = rest[8:22]
    mine, near, part, far = rest[22:26]
    osem, a_s, a_r, b_s, b_r, c_s, c_r, d_s, d_r = rest[26:]
    i = pl.program_id(0)
    G = msg.shape[1]
    spaces = lax.axis_size("space")
    space, rep = lax.axis_index("space"), lax.axis_index("rep")

    down = rep // 2
    ahead = ((space + 1 - 2 * down + spaces) % spaces, rep)
    behind = ((space - 1 + 2 * down + spaces) % spaces, rep)
    slab = lambda m: pl.ds(pl.multiple_of(m * 4 * C, 4 * C), 4 * C)
    edge1 = send(out.at[0], tab0.at[slab(down * (4 - rep // 3))], a_s.at[0], a_r.at[0], ahead)
    edge2 = send(out.at[1], tab0.at[slab(1 + 3 * down)], a_s.at[1], a_r.at[1], ahead)
    ends = rep % 3 == 0
    fill = pltpu.make_async_copy(at_ref, own, osem)
    loads = [pltpu.make_async_copy(a, b, k_sem.at[n]) for n, (a, b) in enumerate(zip(small, kept))]

    def rows_in(g):
        rows = pl.ds(pl.multiple_of(g * G, G), G)
        return [
            pltpu.make_async_copy(b_hbm.at[rows], b_in.at[g], b_sem.at[0, g]),
            pltpu.make_async_copy(cos_hbm.at[rows], cos_in.at[g], b_sem.at[1, g]),
        ]


    def moves(g):
        def rows(m):
            return pl.ds(pl.multiple_of((m * 4 + g) * C, C), C)

        return [
            send(tab1.at[rows(2)], tab1.at[rows(2 - d)], b_s.at[n, g], b_r.at[n, g], beside(d))
            for n, d in enumerate(AROUND)
        ]

    close, away, seat, chip = peers()
    hop1 = [send(mine, near.at[seat], c_s.at[n], c_r.at[n], to) for n, to in enumerate(close)]
    hop2 = [send(part, far.at[chip], d_s.at[n], d_r.at[n], to) for n, to in enumerate(away)]

    greet = [behind] + [beside(d) for d in AROUND] + close + away
    barrier = pltpu.get_barrier_semaphore()

    def count(g):
        return cnt_ref[:, pl.ds(pl.multiple_of(g * G, G), G)]

    def pick(g):
        pairs(bonds.at[g], wpT[...], count(g), PT, QT)

    def gate_weights(layer):
        wcT[...] = (swap(wcore_ref.at[layer], 256) * 0.5).astype(bf)
        waT[...] = swap(watom_ref.at[layer], 128).astype(bf)
        wbT[...] = swap(wbond_ref.at[layer], 128).astype(bf)

    def block(which, dst):
        for n in range(4):
            piece = own[:, pl.ds(pl.multiple_of((which * 4 + n) * G, G), G)]
            dst[n * C : (n + 1) * C, :] = piece.astype(bf)

    @pl.when(i == 0)
    def _():
        for c in loads:
            c.start()
        for g in (1, 2, 3, 0):
            for c in rows_in(g):
                c.start()
            if g == 1:
                fill.start()
        for to in greet:
            pl.semaphore_signal(barrier, inc=1, device_id=to, device_id_type=MESH)
        for c in loads:
            c.wait()
        pair_weights(wp_ref.at[0], wcos_ref, 0, wpT, wb)
        gate_weights(0)
        we[...] = column(we_ref[...], G)
        mine[...] = jnp.zeros_like(mine)

    @pl.when(i == 1)
    def _():
        fill.wait()
        block((1 - down) * (2 + rep), out.at[0])
        block(3 - 2 * down, out.at[1])
        for m in range(5):
            here = rep - 2 + m

            @pl.when((here >= 0) & (here <= 3))
            def _():
                block(here, tab0.at[slab(m)])

        for n in range(4):
            state_of[n] = own[:, pl.ds(pl.multiple_of((rep * 4 + n) * G, G), G)]

    @pl.when(i == 2)
    def _():
        pl.semaphore_wait(barrier, len(greet))
        edge1.start()

        @pl.when(ends)
        def _():
            edge2.start()

    @pl.when(i < 4)
    def _():
        g = (i + 1) % 4
        for c in rows_in(g):
            c.wait()
        for a in range(8):
            bonds[g, a * 128 : (a + 1) * 128, :] = b_in[g, :, a * 128 : (a + 1) * 128].T
        for a in range(2):
            cosT[a * 128 : (a + 1) * 128, :] = cos_in[g, :, a * 128 : (a + 1) * 128].T
        for r in range(S * S):
            if r % (S + 1):
                CB[g, r] = jnp.broadcast_to(cosT[r : r + 1, :], (8, G)).astype(bf)

    @pl.when(i == 3)
    def _():
        pick(0)
        sums(PT, QT, CB.at[0], wb, 1.0 / count(0).astype(f32), sums_of.at[0])
        edge1.wait()

        @pl.when(ends)
        def _():
            edge2.wait()

    @pl.when((i >= 5) & (i <= 8))
    def _():
        for c in moves(i - 5):
            c.start()

    @pl.when((i >= 4) & (i < 7))
    def _():
        pick(i - 3)

    def gates(layer, g, table, ang, hold_gate, beside_it):
        state = state_of[g]
        ctr = state.astype(bf)
        cnt = count(g)
        inv = 1.0 / cnt.astype(f32)
        msg[...] = jnp.zeros_like(msg)
        base = lax.broadcasted_iota(jnp.int32, (1, G), 1) + 2048
        iota = lax.broadcasted_iota(jnp.int32, (256, G), 0).astype(f32).astype(bf)
        one, zero = jnp.ones((256, G), bf), jnp.zeros((256, G), bf)

        def fetch(t):
            which = t // S
            idx = off_ref[pl.ds(t % S, 1), pl.ds(pl.multiple_of(which * G, G), G)] + base
            hi = idx >> 8
            lo = (idx & 255).astype(f32).astype(bf)
            hot = jnp.where(jnp.broadcast_to(lo, (256, G)) == iota, one, zero)
            rows = pl.ds(pl.multiple_of(which * C, C), WIN * C)
            res = jnp.dot(table[rows, :], hot, preferred_element_type=f32)
            hib = jnp.broadcast_to(hi, (C, G))
            nb = res[:C]
            for h in range(1, WIN):
                nb = jnp.where(hib == h, res[h * C : (h + 1) * C], nb)
            return nb.astype(bf)

        def slot(j, nb):
            nxt = fetch(jnp.minimum(g * S + j + 1, 4 * S - 1))
            rows = pl.ds(pl.multiple_of(j * C, C), C)
            mix = bonds[g, rows, :]
            mixed = jnp.dot(wcT[...], jnp.concatenate([ctr, nb, mix], axis=0), preferred_element_type=f32)
            live = jnp.broadcast_to(jnp.where(cnt > j, 0.5, 0.0), (C, G))
            gh, ch, bh = mixed[:C], mixed[C : 2 * C], mixed[2 * C :]
            gl = jnp.tanh(gh) * live + live
            msg[...] += gl * (ch * jnp.tanh(ch) + ch)
            gate = jnp.tanh(bh) * live + live
            if hold_gate:
                sums_of[g - 1, rows, :] = gate.astype(bf)
            else:
                up = jnp.dot(wbT[...], sums_of[ang, rows, :], preferred_element_type=f32)
                bonds[g, rows, :] = (mix.astype(f32) + up * gate).astype(bf)
            beside_it(j)
            return nxt

        @pl.when(g == 0)
        def _():
            nbs[...] = fetch(0)

        nbs[...] = lax.fori_loop(0, S, slot, nbs[...], unroll=UNROLL[layer])
        summed = (msg[...] * inv).astype(bf)
        return state + jnp.dot(waT[...], summed, preferred_element_type=f32)

    def fresh(g, st):
        state_of[g] = st
        tab1[pl.ds(pl.multiple_of((8 + g) * C, C), C), :] = st.astype(bf)

    @pl.when((i >= 4) & (i < 7))
    def _():
        g = i - 4
        inv = 1.0 / count((g + 1) % 4).astype(f32)

        def angle(j):
            angle_slot(j, PT, QT, CB.at[(g + 1) % 4], wb, inv, sums_of.at[g + 1], 2)

        fresh(g, gates(0, g, tab0, g, False, angle))

    @pl.when(i == 7)
    def _():
        fresh(i - 4, gates(1, i - 4, tab0, i - 4, False, lambda j: None))

    @pl.when(i == 8)
    def _():
        pair_weights(wp_ref.at[1], wcos_ref, 1, wpT, wb)
        pick(0)
        sums(PT, QT, CB.at[0], wb, 1.0 / count(0).astype(f32), sums_of.at[4])
        pick(1)
        sums(PT, QT, CB.at[1], wb, 1.0 / count(1).astype(f32), sums_of.at[0])
        gate_weights(1)
        for g in range(4):
            for c in moves(g):
                c.wait()

    def finish(g, st):
        so_ref[...] = st
        e = jnp.sum((st * we[...]).reshape(8, 8, G), axis=0)
        mine[...] += e[:, :128] + e[:, 128:]

    def turn(g):
        for h in range(G // 128):
            for a in range(8):
                cut = bonds[g, a * 128 : (a + 1) * 128, h * 128 : (h + 1) * 128]
                bo_ref[h * 128 : (h + 1) * 128, a * 128 : (a + 1) * 128] = cut.T

    @pl.when((i >= 9) & (i < 11))
    def _():
        g = i - 9
        finish(g, gates(1, g, tab1, 4 - 4 * g, False, lambda j: None))

    @pl.when((i >= 11) & (i < 13))
    def _():
        g = i - 9
        finish(g, gates(1, g, tab1, 0, True, lambda j: None))

    @pl.when(i == 13)
    def _():
        for c in hop1:
            c.start()
        near[seat] = mine[...]

    @pl.when(i >= 13)
    def _():
        g = i - 11
        pick(g)
        sums(PT, QT, CB.at[g], wb, 1.0 / count(g).astype(f32), sums_of.at[3])

    @pl.when(i == 13)
    def _():
        for c in hop1:
            c.wait()
        acc = near[0]
        for n in range(1, near.shape[0]):
            acc = acc + near[n]
        part[...] = acc
        far[chip] = acc
        for c in hop2:
            c.start()

    @pl.when(i >= 13)
    def _():
        g = i - 11
        for j in range(S):
            rows = slice(j * C, (j + 1) * C)
            up = jnp.dot(wbT[...], sums_of[3, rows, :], preferred_element_type=f32)
            new = bonds[g, rows, :].astype(f32) + up * sums_of[g - 1, rows, :].astype(f32)
            bonds[g, rows, :] = new.astype(bf)

    @pl.when(((i >= 9) & (i < 11)) | (i >= 13))
    def _():
        turn(i - 9 - (i // 13) * 2)

    @pl.when(i == 14)
    def _():
        for c in hop2:
            c.wait()
        acc = far[0]
        for n in range(1, far.shape[0]):
            acc = acc + far[n]
        scale = 1.0 / math.sqrt(spaces * lax.axis_size("rep") * 4 * G)
        en_ref[0, 0] = jnp.sum(acc) * scale


def run(bonds, cos, at, *small, G=256):
    two = lambda i: jnp.minimum(jnp.maximum(i - 9, 0), 1)
    sd = jax.ShapeDtypeStruct
    dma = pltpu.SemaphoreType.DMA
    tile = pltpu.VMEM((8, 128), f32)
    chips = lax.axis_size("space") // 2
    seats = 2 * lax.axis_size("rep")
    return pl.pallas_call(
        kernel,
        grid=(15,),
        in_specs=[pl.BlockSpec(memory_space=pltpu.HBM)] * 11,
        out_specs=[
            pl.BlockSpec((C, G), lambda i: (0, jnp.minimum(jnp.maximum(i - 9, 0), 3))),
            pl.BlockSpec((G, 1024), lambda i: (two(i) + (i // 13) * (i - 12), 0)),
            pl.BlockSpec(memory_space=pltpu.SMEM),
        ],
        out_shape=[sd((C, 4 * G), f32), sd((4 * G, 1024), bf), sd((1, 1), f32)],
        scratch_shapes=pair_scratch(G)
        + [pltpu.VMEM((3 * C, 3 * C), bf), pltpu.VMEM((C, C), bf), pltpu.VMEM((C, C), bf), pltpu.VMEM((C, G), f32)]
        + [pltpu.VMEM((C, G), f32), pltpu.VMEM((C, G), bf), pltpu.VMEM((4, 1024, G), bf), pltpu.VMEM((256, G), f32)]
        + [pltpu.VMEM((5, 1024, G), bf), pltpu.VMEM((4, C, G), f32), pltpu.VMEM((20 * C, G), bf)]
        + [pltpu.VMEM((20 * C, G), bf), pltpu.VMEM(at.shape, f32), pltpu.VMEM((2, 4 * C, G), bf)]
        + [tile, pltpu.VMEM((seats, 8, 128), f32), tile, pltpu.VMEM((chips, 8, 128), f32)]
        + [dma, dma((2,)), dma((2,)), dma((4, 4)), dma((4, 4))]
        + [dma((seats - 1,)), dma((seats - 1,)), dma((chips - 1,)), dma((chips - 1,))]
        + [pltpu.VMEM(x.shape, x.dtype) for x in small]
        + [pltpu.VMEM((4, G, 1024), bf), pltpu.VMEM((4, G, 256), f32), dma((8,)), dma((2, 4))],
        compiler_params=pltpu.CompilerParams(collective_id=0, has_side_effects=True),
        name="layers",
    )(bonds, cos, at, *small)


def flush_kernel(st_ref, bonds_ref, so_ref, bo_ref, st, rows, sem):
    n = rows.shape[0]
    size = rows.shape[1]
    ins, outs = [], []
    for k in range(n):
        part = pl.ds(k * size, size)
        ins.append(pltpu.make_async_copy(bonds_ref.at[part], rows.at[k], sem.at[0, k]))
        outs.append(pltpu.make_async_copy(rows.at[k], bo_ref.at[part], sem.at[1, k]))
    ins.append(pltpu.make_async_copy(st_ref, st, sem.at[0, n]))
    outs.append(pltpu.make_async_copy(st, so_ref, sem.at[1, n]))
    for c in ins:
        c.start()
    for c, d in zip(ins, outs):
        c.wait()
        d.start()
    for d in outs:
        d.wait()


def flush(st, bonds, n=8):
    sd = jax.ShapeDtypeStruct
    return pl.pallas_call(
        flush_kernel,
        in_specs=[pl.BlockSpec(memory_space=pl.ANY)] * 2,
        out_specs=[pl.BlockSpec(memory_space=pl.ANY)] * 2,
        out_shape=[sd(st.shape, st.dtype), sd(bonds.shape, bonds.dtype)],
        scratch_shapes=[
            pltpu.VMEM(st.shape, st.dtype),
            pltpu.VMEM((n, bonds.shape[0] // n, bonds.shape[1]), bonds.dtype),
            pltpu.SemaphoreType.DMA((2, n + 1)),
        ],
        name="flush",
    )(st, bonds)


def per_device(atoms, bonds, offsets, counts, cosines, w_core, w_atom, w_pair, w_cos, w_bond, w_energy):
    st, bo, energy = run(
        bonds,
        cosines,
        atoms.T,
        offsets.T,
        counts.reshape(1, -1),
        w_core,
        w_atom,
        w_pair,
        w_cos,
        w_bond,
        w_energy.reshape(1, -1),
    )
    st, bo = flush(st, bo)
    return st.T, bo, energy.reshape(())


def solution(mesh):
    both = ("space", "rep")
    return jax.shard_map(
        per_device,
        mesh=mesh,
        in_specs=(P("space", None), P(both, None), P(both, None), P(both), P(both, None)) + (P(),) * 6,
        out_specs=(P(both, None), P(both, None), P()),
        check_vma=False,
    )
```
